32 devices in a mesh: gx: 8 (over z, y), gy: 4 (over x, core).
Axes of the slice: x: 2, y: 2, z: 4, core: 2. Of those that a mesh axis runs over, the one named last changes fastest.
Arguments:
- cotangent: float32 [2, 128, 1536], P(None, 'gx', 'gy'), may hold values from -12 to 12
- velocity_in: bfloat16 [2, 128, 1536], P(None, 'gx', 'gy'), may hold values from -6 to 6
- hidden_pre1: bfloat16 [64, 128, 1536], P(None, 'gx', 'gy'), may hold values from -6 to 6
- hidden_pre2: bfloat16 [64, 128, 1536], P(None, 'gx', 'gy'), may hold values from -6 to 6
- w_first: bfloat16 [9, 64, 2], replicated, may hold values from -1.5 to 1.5
- w_middle: bfloat16 [9, 64, 64], replicated, may hold values from -0.25 to 0.25
- w_last: bfloat16 [9, 2, 64], replicated, may hold values from -0.25 to 0.25
Outputs:
- grad_velocity: float32 [2, 128, 1536], P(None, 'gx', 'gy')
- grad_first: float32 [9, 64, 2], replicated
- grad_middle: float32 [9, 64, 64], replicated
- grad_last: float32 [9, 2, 64], replicated
- grad_bias1: float32 [64], replicated
- grad_bias2: float32 [64], replicated
The draws below stay inside these ranges and needn't reach their ends.
All inputs are finite; a program needn't handle non-finite values.
Results may differ from the reference program's by a relative error of at most 0.0075.
Values may be sent and summed in bfloat16 or wider, within the bound.
A program may use at most 64 MiB of HBM per device.

```python
import math
import jax
import jax.numpy as jnp
from jax import lax

CH = 64
CX = 16
CY = 384
ITERS = 4
NX = 128
NY = 1536


TWO_PI = 6.283185307179586


def wave_phase(row_wave, col_wave):
    row_index = jnp.arange(NX, dtype=jnp.int32)[:, None]
    col_index = jnp.arange(NY, dtype=jnp.int32)[None, :]
    row_part = (row_wave * row_index % NX).astype(jnp.float32) / NX
    col_part = (col_wave * col_index % NY).astype(jnp.float32) / NY
    return TWO_PI * (row_part + col_part)


def block_levels(key, count, width, lower, upper):
    table = jnp.exp(jax.random.uniform(key, (count // width,), jnp.float32, lower, upper))
    which = jnp.arange(count, dtype=jnp.int32) // width
    return table[which]


def draw_cotangent(key, part):
    keys = jax.random.split(key, 8)
    row_low = max(1, NX // 96)
    row_high = max(row_low, NX // 24) + 1
    col_high = max(1, NY // 24)
    row_waves = jax.random.randint(keys[0], (9,), row_low, row_high)
    col_waves = jax.random.randint(keys[1], (9,), -col_high, col_high + 1)
    phases = jax.random.uniform(keys[2], (9,), jnp.float32, -3.14159, 3.14159)
    amplitudes = jax.random.uniform(keys[3], (8,), jnp.float32, 0.3, 1.2)
    noise = 0.35 * jax.random.truncated_normal(keys[4], -4.0, 4.0, (2, NX, NY), jnp.float32)
    col_noise = block_levels(keys[5], NY, CY, -2.5, 1.5)
    row_noise = block_levels(keys[6], NX, CX, -1.2, 1.2)
    col_smooth = block_levels(keys[7], NY, CY, -1.0, 1.0)
    envelope = jnp.exp(1.15 * jnp.sin(wave_phase(row_waves[8], col_waves[8]) + phases[8]))
    envelope = envelope * row_noise[:, None] * col_noise[None, :]
    components = []
    for comp in range(2):
        smooth = jnp.zeros((NX, NY), jnp.float32)
        for index in range(4):
            which = 4 * comp + index
            smooth = smooth + amplitudes[which] * jnp.sin(wave_phase(row_waves[which], col_waves[which]) + phases[which])
        components.append(smooth * col_smooth[None, :])
    total = jnp.stack(components) + noise * envelope[None, :, :]
    return jnp.clip(total, -12.0, 12.0).astype(jnp.float32)


def level_of(own_key, shape, cuts, least, top_value):
    loudness, own = 1.0, jax.random.fold_in(own_key, 6)
    for axis_at, parts in cuts:
        heights = jnp.exp(jax.random.uniform(jax.random.fold_in(own, axis_at), (parts,), jnp.float32, least / len(cuts), top_value / len(cuts)))
        loudness = loudness * jnp.repeat(heights, shape[axis_at] // parts).reshape([-1 if axis == axis_at else 1 for axis in range(len(shape))])
    return loudness


def bell_draw(key, extent, scale, most, cuts=(), kind=jnp.bfloat16):
    drawn = scale * jax.random.normal(key, extent, jnp.float32)
    if cuts:
        drawn = drawn * level_of(key, extent, cuts, -0.22, 0.18)
    return jnp.clip(drawn, -most, most).astype(kind)


def setup_inputs(seed: int = 0) -> dict:
    arg_keys = jax.random.split(jax.random.key(seed), 8)
    return {
        "cotangent": draw_cotangent(jax.random.fold_in(arg_keys[7], 71), 0),
        "velocity_in": bell_draw(arg_keys[1], (2, NX, NY), 1.0, 6.0, ((1, 8), (2, 4))),
        "hidden_pre1": bell_draw(arg_keys[2], (CH, NX, NY), 1.0, 6.0, ((1, 8), (2, 4))),
        "hidden_pre2": bell_draw(arg_keys[3], (CH, NX, NY), 1.0, 6.0, ((1, 8), (2, 4))),
        "w_first": bell_draw(arg_keys[4], (9, CH, 2), 18 ** -0.5, 1.5),
        "w_middle": bell_draw(arg_keys[5], (9, CH, CH), (9 * CH) ** -0.5, 0.25),
        "w_last": bell_draw(arg_keys[6], (9, 2, CH), (9 * CH) ** -0.5, 0.25),
    }


OFFSETS = ((-1, -1), (-1, 0), (-1, 1), (0, -1), (0, 0), (0, 1), (1, -1), (1, 0), (1, 1))

def moved_to(field, row_step, col_step):
    return jnp.roll(field, (-row_step, -col_step), axis=(1, 2))

def gelu_slope(pre):
    values = pre.astype(jnp.float32)
    _, pullback = jax.vjp(lambda inner: jax.nn.gelu(inner, approximate=True), values)
    return pullback(jnp.ones_like(values))[0]

def apply_stencil(field):
    beside = jnp.roll(field, 2, 0) + jnp.roll(field, -2, 0) + jnp.roll(field, 2, 1)
    beside = beside + jnp.roll(field, -2, 1)
    return field - 0.25 * beside

def conv_back(weights, deltas):
    channels = deltas.shape[0]
    total = jnp.zeros((weights.shape[2], deltas.shape[1] * deltas.shape[2]), jnp.float32)
    for index, (row_step, col_step) in enumerate(OFFSETS):
        shifted = moved_to(deltas, -row_step, -col_step).reshape(channels, -1)
        total = total + lax.dot_general(weights[index], shifted, (((0,), (0,)), ((), ())), preferred_element_type=jnp.float32)
    return total.reshape(weights.shape[2], deltas.shape[1], deltas.shape[2])

def tap_grads(deltas, inputs):
    flat_deltas = deltas.reshape(deltas.shape[0], -1)
    results = []
    for row_step, col_step in OFFSETS:
        shifted = moved_to(inputs, row_step, col_step).reshape(inputs.shape[0], -1)
        results.append(lax.dot_general(flat_deltas, shifted, (((1,), (1,)), ((), ())), preferred_element_type=jnp.float32))
    return jnp.stack(results)

def reference(cotangent, velocity_in, hidden_pre1, hidden_pre2, w_first, w_middle, w_last):
    hidden1 = jax.nn.gelu(hidden_pre1.astype(jnp.float32), approximate=True).astype(jnp.bfloat16)
    hidden2 = jax.nn.gelu(hidden_pre2.astype(jnp.float32), approximate=True).astype(jnp.bfloat16)
    slope1 = gelu_slope(hidden_pre1)
    slope2 = gelu_slope(hidden_pre2)
    along_rows = jnp.roll(cotangent[0], -1, 0) - jnp.roll(cotangent[0], 1, 0)
    along_cols = jnp.roll(cotangent[1], -1, 1) - jnp.roll(cotangent[1], 1, 1)
    rhs = -0.5 * (along_rows + along_cols)
    lam = jnp.zeros_like(rhs)
    residual = rhs
    direction = rhs
    norm_now = jnp.sum(residual * residual)
    for step in range(ITERS):
        image = apply_stencil(direction)
        alpha = norm_now / jnp.sum(direction * image)
        lam = lam + alpha * direction
        if step + 1 < ITERS:
            residual = residual - alpha * image
            norm_next = jnp.sum(residual * residual)
            direction = residual + norm_next / norm_now * direction
            norm_now = norm_next
    adjoint_rows = 0.5 * (jnp.roll(lam, 1, 0) - jnp.roll(lam, -1, 0))
    adjoint_cols = 0.5 * (jnp.roll(lam, 1, 1) - jnp.roll(lam, -1, 1))
    adjoint = cotangent + jnp.stack([adjoint_rows, adjoint_cols])
    adjoint_b = adjoint.astype(jnp.bfloat16)
    delta2 = (conv_back(w_last, adjoint_b) * slope2).astype(jnp.bfloat16)
    delta1 = (conv_back(w_middle, delta2) * slope1).astype(jnp.bfloat16)
    grad_velocity = adjoint + conv_back(w_first, delta1)
    factor = 1.0 / math.sqrt(NX * NY)
    grad_last = factor * tap_grads(adjoint_b, hidden2)
    grad_middle = factor * tap_grads(delta2, hidden1)
    grad_first = factor * tap_grads(delta1, velocity_in)
    grad_bias1 = factor * lax.optimization_barrier(jnp.sum(delta1.astype(jnp.float32), axis=(1, 2)))
    grad_bias2 = factor * lax.optimization_barrier(jnp.sum(delta2.astype(jnp.float32), axis=(1, 2)))
    return (grad_velocity, grad_first, grad_middle, grad_last, grad_bias1, grad_bias2)
```

```python
import functools
import math

import jax
import jax.numpy as jnp
from jax import lax
from jax.experimental import pallas as pl
from jax.experimental.pallas import tpu as pltpu
from jax.sharding import PartitionSpec as P

ITERS = 4
MESH = pl.DeviceIdType.MESH
NEIGHBOURS = tuple((dx, dy) for dx in (-1, 0, 1) for dy in (-1, 0, 1) if (dx, dy) != (0, 0))
NT = (((1,), (1,)), ((), ()))
NN = (((1,), (0,)), ((), ()))
C0 = 0.7978845608028654
C1 = 0.044715


def dot(a, b, dims):
    return lax.dot_general(a, b, dims, preferred_element_type=jnp.float32)


def roll_to(x, shift, axis):
    return pltpu.roll(x, shift % x.shape[axis], axis)


def gelu_both(v):
    square = v * v
    half = 0.5 * (1.0 + jnp.tanh(v * (C0 + (C0 * C1) * square)))
    value = v * half
    return value, half + (value * (1.0 - half)) * (2.0 * C0 + (6.0 * C0 * C1) * square)


def merge_border(block, axis):
    n = block.shape[axis] - 256
    right = lax.slice_in_dim(block, n, n + 128, axis=axis)
    left = lax.slice_in_dim(block, n + 128, n + 256, axis=axis)
    lane = lax.broadcasted_iota(jnp.int32, right.shape, axis)
    border = jnp.where(lane < 64, right, left)
    return jnp.concatenate([lax.slice_in_dim(block, 0, n, axis=axis), border], axis=axis)


def fused_kernel(
    nx, ny, factor, cot_in, vel_in, pre1_in, pre2_in, last_in, taps_in, first_in,
    spread_out, middle_out, last_out, first_out, bias1_out, bias2_out,
    cot, vel, raw, w_lasts, w_taps, w_firsts, natural, rowsend,
    cot_pad, edge_in, halo, slots, grads, sums, gathered, few,
    adj, adj_rolled, vel_rolled, slope1, slope2, hidden1, hidden2, acc, stacks, edges, w_middle, w_last, w_first,
    taps, spread, gm, gl, gf,
    send, recv, load, send_all, recv_all,
):
    rows, cols = cot.shape[1], cot.shape[2]
    ch = raw.shape[1]
    wide = cols + 128
    f32, bf16 = jnp.float32, jnp.bfloat16
    gx, gy = lax.axis_index("gx"), lax.axis_index("gy")
    count = nx * ny
    me = gx * ny + gy

    loads = [
        pltpu.make_async_copy(src, dst, load.at[i])
        for i, (src, dst) in enumerate((
            (pre2_in, raw.at[1]), (pre1_in, raw.at[0]), (cot_in, cot), (taps_in, w_taps), (vel_in, vel),
            (last_in, w_lasts), (first_in, w_firsts),
        ))
    ]
    for copy in loads:
        copy.start()

    def device(k):
        other = lax.rem(me + k, count)
        return other, (lax.div(other, ny), lax.rem(other, ny))

    barrier = pltpu.get_barrier_semaphore()

    def hail(k, _):
        pl.semaphore_signal(barrier, inc=1, device_id=device(k)[1], device_id_type=MESH)
        return 0

    lax.fori_loop(1, count, hail, 0)

    def at(dx, dy):
        return (lax.rem(gx + dx + nx, nx), lax.rem(gy + dy + ny, ny))

    def remote(src, dst, which, index, peer):
        return pltpu.make_async_remote_copy(
            src_ref=src, dst_ref=dst, send_sem=send.at[which, index], recv_sem=recv.at[which, index],
            device_id=peer, device_id_type=MESH,
        )

    def block_copy(src, dst, which, index, dx, dy):
        t = rows * (1 - dx)
        lanes = {1: slice(cols - 128, cols), 0: slice(0, cols), -1: slice(0, 128)}[dy]
        land = {1: slice(cols + 128, cols + 256), 0: slice(0, cols), -1: slice(cols, cols + 128)}[dy]
        return remote(src.at[:, :, lanes], dst.at[:, t : t + rows, land], which, index, at(dx, dy))

    cot_copies = [block_copy(cot, cot_pad, 0, i, dx, dy) for i, (dx, dy) in enumerate(NEIGHBOURS)]
    edge_copies = [
        remote(edges.at[(1 + dy) // 2], edge_in.at[(1 + dy) // 2, 1 - dx], 1, i, at(dx, dy))
        for i, (dx, dy) in enumerate(NEIGHBOURS) if dy
    ]
    row_copies = [
        remote(rowsend.at[0:3], halo.at[0:3], 2, 0, at(1, 0)),
        remote(rowsend.at[3:6], halo.at[3:6], 2, 1, at(-1, 0)),
    ]

    def to_all(which, source, slot):
        def go(k, _):
            other, peer = device(k)
            pltpu.make_async_remote_copy(
                src_ref=source(other), dst_ref=slot.at[me], send_sem=send_all.at[which],
                recv_sem=recv_all.at[which], device_id=peer, device_id_type=MESH,
            ).start()
            return 0

        lax.fori_loop(1, count, go, 0)
        most = slot.at[pl.ds(0, count - 1)]
        return pltpu.make_async_remote_copy(
            src_ref=most, dst_ref=most, send_sem=send_all.at[which], recv_sem=recv_all.at[which],
            device_id=at(0, 1), device_id_type=MESH,
        )

    def total_of(slot):
        total = slot[0]
        for k in range(1, count):
            total = total + slot[k]
        return total

    loads[0].wait()
    loads[1].wait()

    def widen(c, _):
        for which in range(2):
            block = raw[which, c].astype(f32)
            for part in range(cols // 128):
                natural[which, part, pl.ds(c * rows, rows), :] = block[:, 128 * part : 128 * part + 128]
        return 0

    lax.fori_loop(0, ch, widen, 0, unroll=4)

    def row_of(which, part, r):
        return natural[which, part, pl.ds(r, ch, rows), :]

    for i, (which, r) in enumerate(((1, rows - 2), (1, rows - 1), (0, rows - 1), (1, 0), (1, 1), (0, 0))):
        for part in range(cols // 128):
            rowsend[i, :, 128 * part : 128 * part + 128] = row_of(which, part, r).astype(bf16)
    lane = lax.broadcasted_iota(jnp.int32, (ch, 128), 1)
    for side in range(2):
        part = (cols // 128 - 1) * side
        built = jnp.zeros((ch, 128), f32)
        for r in range(rows):
            for which, to_lane in ((1, 2 * r + 4), (0, 2 * r + 66)):
                moved = roll_to(row_of(which, part, r), to_lane - 126 * side, 1)
                built = jnp.where((lane == to_lane) | (lane == to_lane + 1), moved, built)
        edges[side] = built.astype(bf16)

    loads[2].wait()
    pl.semaphore_wait(barrier, count - 1)
    for copy in cot_copies + edge_copies + row_copies:
        copy.start()

    for copy in loads[3:]:
        copy.wait()
    turned = [w_taps[3 * a : 3 * a + 3].astype(f32).reshape(3 * ch, ch) for a in range(3)]
    for a in range(3):
        w_middle[a * ch : (a + 1) * ch, :] = turned[a].T.astype(bf16)
    spread[0] = jnp.zeros_like(spread[0])
    spread[1] = jnp.zeros_like(spread[1])
    for t in range(9):
        spread[0, 2 * t : 2 * t + 2, 0:ch] = w_lasts[t].astype(f32)
        pair = w_firsts[t].astype(f32)
        low = 8 * (t % 3) + 2 * (t // 3)
        spread[1, low : low + 2, 0:ch] = pair
    w_last[...] = spread[0, 0:32, 0:128].T[0:ch].astype(bf16)
    w_first[...] = spread[1, 0:24, 0:ch].astype(bf16)
    cot_pad[:, rows : 2 * rows, 0:cols] = cot[...]
    gm[...] = jnp.zeros_like(gm)
    gl[...] = jnp.zeros_like(gl)
    gf[...] = jnp.zeros_like(gf)
    tap = lax.broadcasted_iota(jnp.int32, (2,) + taps.shape[1:], 1)
    taps[0:2] = jnp.where(tap == 18, 1.0, 0.0)
    taps[2:4] = jnp.zeros((2,) + taps.shape[1:], f32)
    hidden1[0:3] = jnp.zeros((3, ch, cols), bf16)
    hidden1[rows + 3 : rows + 6] = jnp.zeros((3, ch, cols), bf16)
    acc[0:2] = jnp.zeros((2,) + acc.shape[1:], f32)
    vel_rolled[...] = jnp.zeros_like(vel_rolled)
    v = jnp.concatenate([vel[...].astype(f32), jnp.zeros((2, rows, 128), f32)], axis=2)
    for b in (-1, 0, 1):
        for k in range(2):
            vel_rolled[2 * (b + 1) + k, 8 : 8 + rows, :] = roll_to(v[k], -b, 1) if b else v[k]

    def activate(r, _):
        for part in range(cols // 128):
            here = slice(128 * part, 128 * part + 128)
            value, slope = gelu_both(row_of(1, part, r))
            hidden2[r, :, here] = value.astype(bf16)
            slope2[r + 2, :, here] = slope
            value, slope = gelu_both(row_of(0, part, r))
            hidden1[r + 3, :, here] = value.astype(bf16)
            slope1[r + 1, :, here] = slope
        return 0

    lax.fori_loop(0, rows, activate, 0)

    for copy in cot_copies:
        copy.wait_recv()
    c = merge_border(cot_pad[...], 2)
    c0, c1 = c[0], c[1]
    rhs = -0.5 * ((roll_to(c0, -1, 0) - roll_to(c0, 1, 0)) + (roll_to(c1, -1, 1) - roll_to(c1, 1, 1)))
    fields = [rhs]
    for _ in range(ITERS):
        q = fields[-1]
        beside = roll_to(q, 2, 0) + roll_to(q, -2, 0) + roll_to(q, 2, 1)
        fields.append(-0.25 * (beside + roll_to(q, -2, 1)))
    inner = [f[rows : 2 * rows, 0:cols] for f in fields]
    partial = []
    for k in range(2 * ITERS):
        product = inner[k // 2] * inner[(k + 1) // 2]
        total = product[:, 0:128]
        for at_lane in range(128, cols, 128):
            total = total + product[:, at_lane : at_lane + 128]
        partial.append(jnp.sum(total, axis=0, keepdims=True))
    moments = jnp.sum(jnp.concatenate(partial, axis=0), axis=1, keepdims=True)
    square = lax.broadcasted_iota(jnp.int32, (8, 128), 0) == lax.broadcasted_iota(jnp.int32, (8, 128), 1)
    slots[me] = jnp.sum(jnp.where(square, moments, 0.0), axis=0, keepdims=True)
    started = to_all(0, lambda other: slots.at[me], slots)

    for copy in row_copies + edge_copies:
        copy.wait_recv()
    place = lax.rem(lane, 64)
    top = place < jnp.where(lane < 64, 4, 2)
    bottom = place >= jnp.where(lane < 64, 36, 34)
    sides = []
    for side in range(2):
        above, beside, below = (edge_in[side, k].astype(f32) for k in range(3))
        mid = jnp.where(top, pltpu.roll(above, 96, 1), beside)
        sides.append(gelu_both(jnp.where(bottom, pltpu.roll(below, 32, 1), mid))[1])

    def edge_slope(offset):
        return jnp.where(lane < 64, roll_to(sides[0], -offset, 1), roll_to(sides[1], 126 - offset, 1))

    for i in range(rows + 4):
        slope2[i, :, cols : cols + 128] = edge_slope(2 * i)
    for j in range(rows + 2):
        slope1[j, :, cols : cols + 128] = edge_slope(64 + 2 * j)
    for i, row in ((0, 0), (1, 1), (3, rows + 2), (4, rows + 3)):
        slope2[row, :, 0:cols] = gelu_both(halo[i].astype(f32))[1]
    for i, row in ((2, 0), (5, rows + 1)):
        slope1[row, :, 0:cols] = gelu_both(halo[i].astype(f32))[1]

    started.wait_recv()
    moments = jnp.sum(jnp.where(square, jnp.sum(slots[...], axis=0), 0.0), axis=1, keepdims=True)
    n = [moments[k : k + 1, 0:1] for k in range(2 * ITERS)]
    zero, one = jnp.zeros_like(n[0]), jnp.ones_like(n[0])
    lam, residual, direction = [zero] * (ITERS + 1), [one] + [zero] * ITERS, [one] + [zero] * ITERS
    norm_now = n[0]
    for step in range(ITERS):
        product = zero
        for i in range(step + 1):
            for j in range(step + 1):
                product = product + direction[i] * direction[j] * (n[i + j] + n[i + j + 1])
        alpha = norm_now / product
        lam = [x + alpha * p for x, p in zip(lam, direction)]
        if step + 1 < ITERS:
            image = [p + below for p, below in zip(direction, [zero] + direction[:-1])]
            residual = [r - alpha * a for r, a in zip(residual, image)]
            norm_next = zero
            for i in range(step + 2):
                for j in range(step + 2):
                    norm_next = norm_next + residual[i] * residual[j] * n[i + j]
            ratio = norm_next / norm_now
            direction = [r + ratio * p for r, p in zip(residual, direction)]
            norm_now = norm_next
    field = lam[0] * fields[0]
    for k in range(1, ITERS):
        field = field + lam[k] * fields[k]
    adj[0] = c0 + 0.5 * (roll_to(field, 1, 0) - roll_to(field, -1, 0))
    adj[1] = c1 + 0.5 * (roll_to(field, 1, 1) - roll_to(field, -1, 1))
    for b in (-1, 0, 1):
        for k in range(2):
            adj_rolled[2 * (b + 1) + k] = roll_to(adj[k], b, 1) if b else adj[k]

    def gather(which, source, row, sign):
        for t in range(9):
            a, b = t // 3 - 1, t % 3 - 1
            for k in range(2):
                taps[which, 2 * t + k : 2 * t + k + 1, :] = source[2 * (b + 1) + k, pl.ds(row + sign * a, 1), :]

    def first(i, own, needed):
        pair = (i, i + 1)
        for at_pair, row in enumerate(pair):
            gather(at_pair, adj_rolled, rows + row - 2, -1)
        shifted = [taps[at_pair].astype(bf16) for at_pair in range(2)]
        deltas = [(dot(w_last[...], x, NN) * slope2[row]).astype(bf16) for x, row in zip(shifted, pair)]
        for delta, row in zip(deltas, pair):
            wider = delta.astype(f32)
            stacks[row] = jnp.concatenate(
                [roll_to(wider, -1, 1).astype(bf16), delta, roll_to(wider, 1, 1).astype(bf16)], axis=0
            )
        for at_pair in needed:
            right = hidden1[pl.ds(pair[at_pair], 3)].reshape(3 * ch, cols)
            gm[...] += dot(stacks[pair[at_pair], :, 0:cols], right, NT)
        if own:
            both = [jnp.concatenate([hidden2[row - 2], d[:, 0:cols]], axis=0) for row, d in zip(pair, deltas)]
            gl[...] += dot(shifted[0][:, 0:cols], both[0], NT) + dot(shifted[1][:, 0:cols], both[1], NT)
        return 0

    first(0, False, (1,))
    lax.fori_loop(0, rows // 2, lambda k, _: first(2 * k + 2, True, (0, 1)), 0)
    first(rows + 2, False, (0,))
    half = 9 * ch // 2
    chunk = grads.shape[1]
    third = 3 * ch // 2
    packed = jnp.concatenate([gm[0:third, 128:192], gm[third : 2 * third, 128:192]], axis=1)
    packed = jnp.concatenate(
        [gm[:, 0:128], packed, gl[0:24], jnp.zeros((count * chunk - half - 24, 128), f32)], axis=0
    )
    for k in range(count):
        grads[k] = packed[k * chunk : (k + 1) * chunk]
    sums[me] = grads[me]
    scatter = to_all(1, lambda other: grads.at[other], sums)

    def middle(k, _):
        i = 2 * k
        y, z = (dot(w_middle[...], stacks[i + at_pair], NN) for at_pair in range(2))
        acc[i] += y[0:ch]
        acc[i + 1] += y[ch : 2 * ch] + z[0:ch]
        acc[i + 2] = y[2 * ch : 3 * ch] + z[ch : 2 * ch]
        acc[i + 3] = z[2 * ch : 3 * ch]
        return 0

    lax.fori_loop(0, rows // 2 + 2, middle, 0)
    spread[...] = jnp.zeros_like(spread)

    def second(pair):
        deltas = [(acc[j + 2] * slope1[j]).astype(bf16) for j in pair]
        products = [dot(w_first[...], x, NN) for x in deltas]
        for at_pair, j in enumerate(pair):
            gather(2 + at_pair, vel_rolled, 7 + j, 1)
        taken = [taps[2 + at_pair].astype(bf16) for at_pair in range(2)]
        gf[...] += dot(taken[0], deltas[0], NT) + dot(taken[1], deltas[1], NT)
        for j, e in zip(pair, products):
            f = roll_to(e[0:8], -1, 1) + e[8:16] + roll_to(e[16:24], 1, 1)
            f = f[:, 0:cols]
            for a in (-1, 0, 1):
                for k in range(2):
                    row = 2 * (a + 1) + k
                    spread[k, pl.ds(j + 1 + a, 1), :] += f[row : row + 1, :]
        return 0

    second((0, rows + 1))
    mine = jnp.where(lax.broadcasted_iota(jnp.int32, (1, wide), 1) < cols, 1.0, 0.0)
    for at_pair in range(2):
        taps[2 + at_pair, 18:19, :] = mine
    lax.fori_loop(0, rows // 4, lambda k, _: second((2 * k + 1, 2 * k + 2)), 0)
    scatter.wait_recv()
    gathered[me] = factor * total_of(sums)
    spreading = to_all(2, lambda other: gathered.at[me], gathered)
    lax.fori_loop(rows // 4, rows // 2, lambda k, _: second((2 * k + 1, 2 * k + 2)), 0)
    few[me] = jnp.concatenate([gf[0:12], gf[12:24]], axis=1)
    last = to_all(3, lambda other: few.at[me], few)
    for k in range(2):
        spread_out[k] = adj[k, rows : 2 * rows, 0:cols] + spread[k, 2 : rows + 2, :]
    for copy in cot_copies + edge_copies + row_copies:
        copy.wait_send()
    started.wait_send()
    scatter.wait_send()
    spreading.wait_recv()
    spreading.wait_send()
    whole = jnp.concatenate([gathered[k] for k in range(count)], axis=0)
    for t in range(9):
        a, start = t // 3, (t % 3) * ch
        for low in range(0, ch, 32):
            here = start + low
            side = a * ch
            if a == 2:
                side = 0 if here < third else 64
                here = 3 * ch + here % third
            middle_out[t, low : low + 32, :] = whole[here : here + 32, side : side + ch]
    for t in range(9):
        last_out[t] = whole[half + 2 * t : half + 2 * t + 2, 0:ch]
    bias2_out[...] = whole[half + 18 : half + 19, ch : 2 * ch]
    last.wait_recv()
    last.wait_send()
    summed = factor * total_of(few)
    summed = jnp.concatenate([summed[:, 0:ch], summed[:, ch : 2 * ch]], axis=0)
    for t in range(9):
        first_out[t] = summed[2 * t : 2 * t + 2]
    bias1_out[...] = summed[18:19]


def store_kernel(*refs):
    count = (len(refs) - 1) // 2
    copies = [
        pltpu.make_async_copy(refs[i], refs[count + i], refs[-1].at[i]) for i in range(count)
    ]
    for copy in copies:
        copy.start()
    for copy in copies:
        copy.wait()


def per_device(nx, ny, cotangent, velocity_in, hidden_pre1, hidden_pre2, w_first, w_middle, w_last):
    rows, cols = cotangent.shape[1], cotangent.shape[2]
    ch = hidden_pre1.shape[0]
    f32, bf16 = jnp.float32, jnp.bfloat16
    factor = 1.0 / math.sqrt(rows * nx * cols * ny)
    vmem = pl.BlockSpec(memory_space=pltpu.VMEM)
    anywhere = pl.BlockSpec(memory_space=pl.ANY)
    dma = pltpu.SemaphoreType.DMA
    count = nx * ny
    packed = 9 * ch // 2 + 24
    chunk = -(-packed // count)
    wide = cols + 128
    out_shapes = (
        jax.ShapeDtypeStruct((2, rows, cols), f32),
        jax.ShapeDtypeStruct((9, ch, ch), f32),
        jax.ShapeDtypeStruct((9, 2, ch), f32),
        jax.ShapeDtypeStruct((9, 2, ch), f32),
        jax.ShapeDtypeStruct((1, ch), f32),
        jax.ShapeDtypeStruct((1, ch), f32),
    )
    results = pl.pallas_call(
        functools.partial(fused_kernel, nx, ny, factor),
        out_shape=out_shapes,
        in_specs=[anywhere] * 7,
        out_specs=(vmem,) * 6,
        scratch_shapes=[
            pltpu.VMEM((2, rows, cols), f32),
            pltpu.VMEM((2, rows, cols), bf16),
            pltpu.VMEM((2, ch, rows, cols), bf16),
            pltpu.VMEM((9, 2, ch), bf16),
            pltpu.VMEM((9, ch, ch), bf16),
            pltpu.VMEM((9, 2, ch), bf16),
            pltpu.VMEM((2, cols // 128, ch * rows, 128), f32),
            pltpu.VMEM((6, ch, cols), bf16),
            pltpu.VMEM((2, 3 * rows, cols + 256), f32),
            pltpu.VMEM((2, 3, ch, 128), bf16),
            pltpu.VMEM((6, ch, cols), bf16),
            pltpu.VMEM((count, 1, 128), f32),
            pltpu.VMEM((count, chunk, 128), f32),
            pltpu.VMEM((count, chunk, 128), f32),
            pltpu.VMEM((count, chunk, 128), f32),
            pltpu.VMEM((count, 12, 128), f32),
            pltpu.VMEM((2, 3 * rows, wide), f32),
            pltpu.VMEM((6, 3 * rows, wide), f32),
            pltpu.VMEM((6, rows + 16, wide), f32),
            pltpu.VMEM((rows + 2, ch, wide), f32),
            pltpu.VMEM((rows + 4, ch, wide), f32),
            pltpu.VMEM((rows + 6, ch, cols), bf16),
            pltpu.VMEM((rows, ch, cols), bf16),
            pltpu.VMEM((rows + 6, ch, wide), f32),
            pltpu.VMEM((rows + 4, 3 * ch, wide), bf16),
            pltpu.VMEM((2, ch, 128), bf16),
            pltpu.VMEM((3 * ch, 3 * ch), bf16),
            pltpu.VMEM((ch, 32), bf16),
            pltpu.VMEM((24, ch), bf16),
            pltpu.VMEM((4, 32, wide), f32),
            pltpu.VMEM((2, max(rows + 8, 32), cols), f32),
            pltpu.VMEM((3 * ch, 3 * ch), f32),
            pltpu.VMEM((32, 2 * ch), f32),
            pltpu.VMEM((32, ch), f32),
            dma((3, 8)), dma((3, 8)), dma((7,)), dma((4,)), dma((4,)),
        ],
        compiler_params=pltpu.CompilerParams(
            collective_id=0, has_side_effects=True, vmem_limit_bytes=56 * 2**20
        ),
    )(
        cotangent, velocity_in, hidden_pre1, hidden_pre2, w_last, w_middle, jnp.transpose(w_first, (0, 2, 1)),
    )
    grad_velocity, grad_middle, grad_last, grad_first, bias1, bias2 = pl.pallas_call(
        store_kernel,
        out_shape=out_shapes,
        in_specs=[vmem] * 6,
        out_specs=(anywhere,) * 6,
        scratch_shapes=[dma((6,))],
    )(*results)
    grad_first = jnp.transpose(grad_first, (0, 2, 1))
    return grad_velocity, grad_first, grad_middle, grad_last, bias1.reshape(ch), bias2.reshape(ch)


def solution(mesh):
    whole = P(None, "gx", "gy")
    return jax.shard_map(
        functools.partial(per_device, mesh.shape["gx"], mesh.shape["gy"]),
        mesh=mesh,
        in_specs=(whole, whole, whole, whole, P(), P(), P()),
        out_specs=(whole, P(), P(), P(), P(), P()),
        check_vma=False,
    )
```

```python
import functools
import math

import jax
import jax.numpy as jnp
from jax import lax
from jax.experimental import pallas as pl
from jax.experimental.pallas import tpu as pltpu
from jax.sharding import PartitionSpec as P

ITERS = 4
MESH = pl.DeviceIdType.MESH
NEIGHBOURS = tuple((dx, dy) for dx in (-1, 0, 1) for dy in (-1, 0, 1) if (dx, dy) != (0, 0))
NT = (((1,), (1,)), ((), ()))
NN = (((1,), (0,)), ((), ()))
C0 = 0.7978845608028654
C1 = 0.044715


def dot(a, b, dims):
    return lax.dot_general(a, b, dims, preferred_element_type=jnp.float32)


def roll_to(x, shift, axis):
    return pltpu.roll(x, shift % x.shape[axis], axis)


def gelu_both(v):
    square = v * v
    half = 0.5 * (1.0 + jnp.tanh(v * (C0 + (C0 * C1) * square)))
    value = v * half
    return value, half + (value * (1.0 - half)) * (2.0 * C0 + (6.0 * C0 * C1) * square)


def fused_kernel(
    nx, ny, factor, cot_in, vel_in, pre1_in, pre2_in, last_in, taps_in, first_in,
    spread_out, middle_out, last_out, first_out, bias1_out, bias2_out,
    cot, cot_edge, cot_side, vel, raw, w_lasts, w_taps, w_firsts, natural, rowsend, halo, edges, edge_in,
    slots, grads, sums, gathered, few, adj, vel_wide, vel_band, slope1, slope2, hidden2, hidden3, stacks, partial,
    deltas, w_middle, w_last, w_first, small, gm, border, side_out, row_in, corner_in, side_in,
    send, recv, load, send_all, recv_all,
):
    rows, cols = vel.shape[1], vel.shape[2]
    ch = raw.shape[1]
    wide = cols + 128
    blocks = cols // 128
    band = rows + 16
    f32, bf16 = jnp.float32, jnp.bfloat16
    gx, gy = lax.axis_index("gx"), lax.axis_index("gy")
    count = nx * ny
    me = gx * ny + gy

    loads = [
        pltpu.make_async_copy(src, dst, load.at[i])
        for i, (src, dst) in enumerate((
            (pre2_in, raw.at[1]), (pre1_in, raw.at[0]), (cot_in, cot.at[:, rows : 2 * rows]), (vel_in, vel),
            (taps_in, w_taps), (last_in, w_lasts), (first_in, w_firsts),
        ))
    ]
    for copy in loads:
        copy.start()

    def device(k):
        other = lax.rem(me + k, count)
        return other, (lax.div(other, ny), lax.rem(other, ny))

    barrier = pltpu.get_barrier_semaphore()

    def hail(k, _):
        pl.semaphore_signal(barrier, inc=1, device_id=device(k)[1], device_id_type=MESH)
        return 0

    lax.fori_loop(1, count, hail, 0)

    def at(dx, dy):
        return (lax.rem(gx + dx + nx, nx), lax.rem(gy + dy + ny, ny))

    def remote(src, dst, which, index, peer):
        return pltpu.make_async_remote_copy(
            src_ref=src, dst_ref=dst, send_sem=send.at[which, index], recv_sem=recv.at[which, index],
            device_id=peer, device_id_type=MESH,
        )

    own = slice(rows, 2 * rows)
    cot_copies, edge_copies, back_copies = [], [], []
    for i, (dx, dy) in enumerate(NEIGHBOURS):
        t = rows * (1 - dx)
        side = (1 + dy) // 2
        if dy:
            cot_copies.append(
                remote(cot_edge.at[side], cot_side.at[side, t : t + rows], 0, i, at(dx, dy))
            )
            edge_copies.append(remote(edges.at[side], edge_in.at[side, 1 - dx], 1, i, at(dx, dy)))
        else:
            cot_copies.append(remote(cot.at[:, own], cot.at[:, t : t + rows], 0, i, at(dx, dy)))
        down = (1 + dx) // 2
        if dx and dy:
            back_copies.append(
                remote(border.at[down, :, :, cols:wide], corner_in.at[down, side], 3, i, at(dx, dy))
            )
        elif dx:
            back_copies.append(remote(border.at[down, :, :, 0:cols], row_in.at[down], 3, i, at(dx, dy)))
        else:
            back_copies.append(remote(side_out, side_in.at[side], 3, i, at(dx, dy)))
    row_copies = [remote(rowsend.at[0], halo.at[0], 2, 0, at(1, 0)), remote(rowsend.at[1], halo.at[1], 2, 1, at(-1, 0))]

    def to_all(which, source, slot):
        def go(k, _):
            other, peer = device(k)
            pltpu.make_async_remote_copy(
                src_ref=source(other), dst_ref=slot.at[me], send_sem=send_all.at[which],
                recv_sem=recv_all.at[which], device_id=peer, device_id_type=MESH,
            ).start()
            return 0

        lax.fori_loop(1, count, go, 0)
        most = slot.at[pl.ds(0, count - 1)]
        return pltpu.make_async_remote_copy(
            src_ref=most, dst_ref=most, send_sem=send_all.at[which], recv_sem=recv_all.at[which],
            device_id=at(0, 1), device_id_type=MESH,
        )

    def total_of(slot):
        total = slot[0]
        for k in range(1, count):
            total = total + slot[k]
        return total

    def iota(shape, axis):
        return lax.broadcasted_iota(jnp.int32, shape, axis)

    loads[2].wait()
    lane = iota((rows, 128), 1)
    c_first = [cot[k, own, 0:128] for k in range(2)]
    c_last = [cot[k, own, cols - 128 : cols] for k in range(2)]
    cot_edge[0] = jnp.where(lane < 16, c_first[0], roll_to(c_first[1], 16, 1))
    cot_edge[1] = jnp.where(lane < 112, roll_to(c_last[1], -16, 1), c_last[0])
    loads[0].wait()
    loads[1].wait()

    def widen(c, _):
        for which in range(2):
            block = raw[which, c].astype(f32)
            for part in range(blocks):
                natural[which, part, pl.ds(c * rows, rows), :] = block[:, 128 * part : 128 * part + 128]
        return 0

    lax.fori_loop(0, ch, widen, 0, unroll=4)

    def row_of(which, part, r):
        return natural[which, part, pl.ds(r, ch, rows), :]

    loads[3].wait()
    v = vel[...].astype(f32)
    for i, r in enumerate((rows - 1, 0)):
        for part in range(blocks):
            rowsend[i, 0:ch, 128 * part : 128 * part + 128] = row_of(1, part, r).astype(bf16)
        pair = jnp.concatenate([v[0, r : r + 1], v[1, r : r + 1], jnp.zeros((14, cols), f32)], axis=0)
        rowsend[i, ch : ch + 16, :] = pair.astype(bf16)
    lane = iota((ch, 128), 1)
    placed = iota((rows, 128), 1) == iota((rows, 128), 0) + 1
    for side in range(2):
        built = jnp.zeros((ch, 128), f32)
        for r in range(rows):
            moved = roll_to(row_of(1, (blocks - 1) * side, r), r + 1 + side, 1)
            built = jnp.where(lane == r + 1, moved, built)
        edges[side, 0:ch, :] = built.astype(bf16)
        col = (cols - 1) * side
        ends = [
            jnp.sum(jnp.where(placed, v[k, :, col : col + 1], 0.0), axis=0, keepdims=True) for k in range(2)
        ]
        edges[side, ch : ch + 16, :] = jnp.concatenate(ends + [jnp.zeros((14, 128), f32)], axis=0).astype(bf16)

    pl.semaphore_wait(barrier, count - 1)
    for copy in cot_copies + row_copies + edge_copies:
        copy.start()

    for copy in loads[4:]:
        copy.wait()
    turned = [w_taps[3 * a : 3 * a + 3].astype(f32).reshape(3 * ch, ch) for a in range(3)]
    for a in range(3):
        w_middle[a * ch : (a + 1) * ch, :] = turned[a].T.astype(bf16)
    small[...] = jnp.zeros_like(small)
    for t in range(9):
        small[0, 2 * t : 2 * t + 2, 0:ch] = w_lasts[t].astype(f32)
        small[1, 2 * t : 2 * t + 2, 0:ch] = w_firsts[t].astype(f32)
    taps = iota((32, 256), 0)
    place = iota((32, 256), 1)
    spot = jnp.where((taps < 18) & (place == band * lax.rem(taps, 6) + 8 - lax.div(taps, 6)), 1.0, 0.0)
    w_turned = small[0].T[0:ch, 0:32].astype(bf16)
    base = dot(w_turned, spot.astype(bf16), NN)
    for i in range(rows + 2):
        w_last[i * ch : (i + 1) * ch, :] = (roll_to(base, i, 1) if i else base).astype(bf16)
    taps = iota((256, 32), 1)
    place = iota((256, 32), 0)
    spot = jnp.where((taps < 18) & (place == band * lax.rem(taps, 6) + 7 + lax.div(taps, 6)), 1.0, 0.0)
    base = dot(spot.astype(bf16), small[1, 0:32, 0:ch].astype(bf16), NN)[0 : 6 * band]
    for j in range(0, rows, 2):
        w_first[:, j * ch : (j + 2) * ch] = jnp.concatenate(
            [roll_to(base, j, 0) if j else base, roll_to(base, j + 1, 0)], axis=1
        ).astype(bf16)
    gm[...] = jnp.zeros_like(gm)
    for i, a in ((0, 0), (0, 1), (1, 0), (rows, 2), (rows + 1, 1), (rows + 1, 2)):
        hidden3[i, a * ch : (a + 1) * ch, :] = jnp.zeros((ch, cols), bf16)
    one_row = jnp.where(iota((16, cols), 0) == 0, 1.0, 0.0).astype(bf16)
    for i in range(rows + 2):
        hidden3[i, 3 * ch : 3 * ch + 16, :] = one_row if 0 < i <= rows else jnp.zeros((16, cols), bf16)

    def activate(r, _):
        for part in range(blocks):
            here = slice(128 * part, 128 * part + 128)
            value, slope = gelu_both(row_of(1, part, r))
            hidden2[r, :, here] = value.astype(bf16)
            slope2[r + 1, :, here] = slope
            value, slope = gelu_both(row_of(0, part, r))
            value = value.astype(bf16)
            for a in range(3):
                hidden3[r + 2 - a, a * ch : (a + 1) * ch, here] = value
            slope1[r, :, here] = slope
        return 0

    lax.fori_loop(0, rows, activate, 0)

    for copy in cot_copies:
        copy.wait_recv()
    tall = iota((3 * rows, 128), 1) < 64
    from_right, from_left = cot_side[0], cot_side[1]
    sides = [
        jnp.where(tall, from_right, from_left),
        jnp.where(tall, roll_to(from_right, -16, 1), roll_to(from_left, 16, 1)),
    ]
    c0, c1 = (jnp.concatenate([cot[k], sides[k]], axis=1) for k in range(2))
    rhs = -0.5 * ((roll_to(c0, -1, 0) - roll_to(c0, 1, 0)) + (roll_to(c1, -1, 1) - roll_to(c1, 1, 1)))
    fields = [rhs]
    for _ in range(ITERS):
        q = fields[-1]
        beside = roll_to(q, 2, 0) + roll_to(q, -2, 0) + roll_to(q, 2, 1)
        fields.append(-0.25 * (beside + roll_to(q, -2, 1)))
    inner = [f[own, 0:cols] for f in fields]
    parts = []
    for k in range(2 * ITERS):
        product = inner[k // 2] * inner[(k + 1) // 2]
        total = product[:, 0:128]
        for at_lane in range(128, cols, 128):
            total = total + product[:, at_lane : at_lane + 128]
        parts.append(jnp.sum(total, axis=0, keepdims=True))
    moments = jnp.sum(jnp.concatenate(parts, axis=0), axis=1, keepdims=True)
    square = iota((8, 128), 0) == iota((8, 128), 1)
    slots[me] = jnp.sum(jnp.where(square, moments, 0.0), axis=0, keepdims=True)
    started = to_all(0, lambda other: slots.at[me], slots)

    for copy in row_copies + edge_copies:
        copy.wait_recv()
    tall = iota((ch + 16, 128), 1)
    merged = []
    for side in range(2):
        above, beside, below = (edge_in[side, k].astype(f32) for k in range(3))
        mid = jnp.where(tall < 1, roll_to(above, -rows, 1), beside)
        merged.append(jnp.where(tall > rows, roll_to(below, rows, 1), mid))
    bent = [gelu_both(m[0:ch])[1] for m in merged]
    for i in range(rows + 2):
        slope2[i, :, cols:wide] = jnp.where(
            lane < 64, roll_to(bent[0], -i, 1) if i else bent[0], roll_to(bent[1], 127 - i, 1)
        )
    for i, row in enumerate((0, rows + 1)):
        slope2[row, :, 0:cols] = gelu_both(halo[i, 0:ch].astype(f32))[1]
    vel_wide[...] = jnp.zeros_like(vel_wide)
    vel_wide[:, 8 : 8 + rows, 0:cols] = v
    upright = [roll_to(m[ch : ch + 16].T[0:band], 7, 0) for m in merged]
    at_lane = iota((band, 128), 1)
    for k in range(2):
        vel_wide[k, :, cols:wide] = jnp.where(at_lane == 0, upright[0][:, k : k + 1], 0.0) + jnp.where(
            at_lane == 127, upright[1][:, k : k + 1], 0.0
        )
        for i, row in enumerate((7, 8 + rows)):
            vel_wide[k, row : row + 1, 0:cols] = halo[i, ch : ch + 16].astype(f32)[k : k + 1]
    for b in (-1, 0, 1):
        for k in range(2):
            at_band = band * (2 * (b + 1) + k)
            moved = roll_to(vel_wide[k], -b, 1) if b else vel_wide[k]
            vel_band[at_band : at_band + band, :] = moved[:, 0:cols].astype(bf16)
    vel_band[6 * band : 256, :] = jnp.where(iota((256 - 6 * band, cols), 0) < rows, 1.0, 0.0).astype(bf16)

    started.wait_recv()
    moments = jnp.sum(jnp.where(square, jnp.sum(slots[...], axis=0), 0.0), axis=1, keepdims=True)
    n = [moments[k : k + 1, 0:1] for k in range(2 * ITERS)]
    zero, one = jnp.zeros_like(n[0]), jnp.ones_like(n[0])
    lam, residual, direction = [zero] * (ITERS + 1), [one] + [zero] * ITERS, [one] + [zero] * ITERS
    norm_now = n[0]
    for step in range(ITERS):
        product = zero
        for i in range(step + 1):
            for j in range(step + 1):
                product = product + direction[i] * direction[j] * (n[i + j] + n[i + j + 1])
        alpha = norm_now / product
        lam = [x + alpha * p for x, p in zip(lam, direction)]
        if step + 1 < ITERS:
            image = [p + below for p, below in zip(direction, [zero] + direction[:-1])]
            residual = [r - alpha * a for r, a in zip(residual, image)]
            norm_next = zero
            for i in range(step + 2):
                for j in range(step + 2):
                    norm_next = norm_next + residual[i] * residual[j] * n[i + j]
            ratio = norm_next / norm_now
            direction = [r + ratio * p for r, p in zip(residual, direction)]
            norm_now = norm_next
    field = lam[0] * fields[0]
    for k in range(1, ITERS):
        field = field + lam[k] * fields[k]
    low = rows - 8
    a0 = (c0 + 0.5 * (roll_to(field, 1, 0) - roll_to(field, -1, 0)))[low : low + band]
    a1 = (c1 + 0.5 * (roll_to(field, 1, 1) - roll_to(field, -1, 1)))[low : low + band]
    adj[0] = a0[8 : 8 + rows, 0:cols]
    adj[1] = a1[8 : 8 + rows, 0:cols]
    banded = jnp.concatenate(
        [roll_to(x, b, 1) if b else x for b in (-1, 0, 1) for x in (a0, a1)]
        + [jnp.zeros((256 - 6 * band, wide), f32)],
        axis=0,
    ).astype(bf16)

    for i in range(0, rows + 2, 2):
        flat = dot(w_last[i * ch : (i + 2) * ch, :], banded, NN)
        for at_pair in range(2):
            delta = flat[at_pair * ch : (at_pair + 1) * ch] * slope2[i + at_pair]
            for s, b in enumerate((-1, 0, 1)):
                moved = roll_to(delta, b, 1) if b else delta
                stacks[i + at_pair, s * ch : (s + 1) * ch, :] = moved[:, 0:cols].astype(bf16)
        gm[...] += dot(
            jnp.concatenate([stacks[i], stacks[i + 1]], axis=1),
            jnp.concatenate([hidden3[i], hidden3[i + 1]], axis=1), NT,
        )

    def fold(source, other):
        flat = dot(source[...].reshape(rows * ch, cols), other, NT)
        total = flat[0:ch]
        for r in range(1, rows):
            total = total + roll_to(flat[r * ch : (r + 1) * ch], -r, 1)
        return total

    def pick(target, turned, sign):
        for m in range(19):
            row = 6 * band if m == 18 else band * (m % 6) + 8 + sign * (m // 6 - 1)
            half = slice(0, ch) if m < 12 else slice(ch, 2 * ch)
            target[m % 12 : m % 12 + 1, half] = turned[row : row + 1, 0:ch]

    gl = fold(hidden2, banded[:, 0:cols])
    gl = jnp.where(iota((ch, 256), 1) == 6 * band, gm[ch : 2 * ch, 3 * ch : 3 * ch + 1], gl)
    small[0] = jnp.zeros_like(small[0])
    pick(small.at[0], gl.T, -1)
    half = 9 * ch // 2
    chunk = grads.shape[1]
    third = 3 * ch // 2
    packed = jnp.concatenate([gm[0:third, 128:192], gm[third : 2 * third, 128:192]], axis=1)
    packed = jnp.concatenate(
        [gm[:, 0:128], packed, small[0, 0:16, :], jnp.zeros((count * chunk - half - 16, 128), f32)], axis=0
    )
    for k in range(count):
        grads[k] = packed[k * chunk : (k + 1) * chunk]
    sums[me] = grads[me]
    scatter = to_all(1, lambda other: grads.at[other], sums)

    for i in range(0, rows + 2, 2):
        flat = dot(w_middle[...], jnp.concatenate([stacks[i], stacks[i + 1]], axis=1), NN)
        partial[i] = flat[:, 0:cols]
        partial[i + 1] = flat[:, cols : 2 * cols]
    for j in range(rows):
        total = partial[j + 2, 0:ch] + partial[j + 1, ch : 2 * ch] + partial[j, 2 * ch : 3 * ch]
        deltas[j] = (total * slope1[j]).astype(bf16)
    gf = fold(deltas, vel_band[...])
    few[me] = jnp.zeros((12, 128), f32)
    pick(few.at[me], gf.T, 1)
    last = to_all(3, lambda other: few.at[me], few)
    flat = dot(w_first[...], deltas[...].reshape(rows * ch, cols), NN)
    flat = jnp.concatenate([flat, jnp.zeros((6 * band, 128), f32)], axis=1)
    spread = []
    for k in range(2):
        terms = [flat[band * (2 * s + k) : band * (2 * s + k + 1)] for s in range(3)]
        spread.append(roll_to(terms[0], -1, 1) + terms[1] + roll_to(terms[2], 1, 1))
        border[0, k] = spread[k][7:8]
        border[1, k] = spread[k][8 + rows : 9 + rows]
        side_out[k] = spread[k][8 : 8 + rows, cols:wide]
    for copy in back_copies:
        copy.start()
    for k in range(2):
        spread_out[k] = adj[k] + spread[k][8 : 8 + rows, 0:cols]
    for copy in cot_copies + edge_copies + row_copies:
        copy.wait_send()
    started.wait_send()

    scatter.wait_recv()
    gathered[me] = factor * total_of(sums)
    spreading = to_all(2, lambda other: gathered.at[me], gathered)
    for copy in back_copies:
        copy.wait_recv()
    for copy in back_copies:
        copy.wait_send()
    left = iota((1, 128), 1) == 0
    right = iota((1, 128), 1) == 127
    for k in range(2):
        spread_out[k, :, 0:128] += jnp.where(left, side_in[1, k], 0.0)
        spread_out[k, :, cols - 128 : cols] += jnp.where(right, side_in[0, k], 0.0)
        for down, row in ((1, 0), (0, rows - 1)):
            spread_out[k, row : row + 1, :] += row_in[down, k]
            spread_out[k, row : row + 1, 0:128] += jnp.where(left, corner_in[down, 1, k], 0.0)
            spread_out[k, row : row + 1, cols - 128 : cols] += jnp.where(right, corner_in[down, 0, k], 0.0)
    last.wait_recv()
    summed = factor * total_of(few)
    for t in range(9):
        for k in range(2):
            m = 2 * t + k
            low = ch * (m // 12)
            first_out[t, k : k + 1] = summed[m % 12 : m % 12 + 1, low : low + ch]
    bias1_out[...] = summed[6:7, ch : 2 * ch]
    scatter.wait_send()
    last.wait_send()
    spreading.wait_recv()
    spreading.wait_send()
    whole = jnp.concatenate([gathered[k] for k in range(count)], axis=0)
    for t in range(9):
        a, start = t // 3, (t % 3) * ch
        for low in range(0, ch, 32):
            here = start + low
            side = a * ch
            if a == 2:
                side = 0 if here < third else 64
                here = 3 * ch + here % third
            middle_out[t, low : low + 32, :] = whole[here : here + 32, side : side + ch]
    for t in range(9):
        for k in range(2):
            m = 2 * t + k
            low, row = ch * (m // 12), half + m % 12
            last_out[t, k : k + 1] = whole[row : row + 1, low : low + ch]
    bias2_out[...] = whole[half + 6 : half + 7, ch : 2 * ch]


def store_kernel(*refs):
    count = (len(refs) - 1) // 2
    copies = [
        pltpu.make_async_copy(refs[i], refs[count + i], refs[-1].at[i]) for i in range(count)
    ]
    for copy in copies:
        copy.start()
    for copy in copies:
        copy.wait()


def per_device(nx, ny, cotangent, velocity_in, hidden_pre1, hidden_pre2, w_first, w_middle, w_last):
    rows, cols = cotangent.shape[1], cotangent.shape[2]
    ch = hidden_pre1.shape[0]
    f32, bf16 = jnp.float32, jnp.bfloat16
    factor = 1.0 / math.sqrt(rows * nx * cols * ny)
    vmem = pl.BlockSpec(memory_space=pltpu.VMEM)
    anywhere = pl.BlockSpec(memory_space=pl.ANY)
    dma = pltpu.SemaphoreType.DMA
    count = nx * ny
    packed = 9 * ch // 2 + 16
    chunk = -(-packed // count)
    wide, band = cols + 128, rows + 16
    out_shapes = (
        jax.ShapeDtypeStruct((2, rows, cols), f32),
        jax.ShapeDtypeStruct((9, ch, ch), f32),
        jax.ShapeDtypeStruct((9, 2, ch), f32),
        jax.ShapeDtypeStruct((9, 2, ch), f32),
        jax.ShapeDtypeStruct((1, ch), f32),
        jax.ShapeDtypeStruct((1, ch), f32),
    )
    results = pl.pallas_call(
        functools.partial(fused_kernel, nx, ny, factor),
        out_shape=out_shapes,
        in_specs=[anywhere] * 7,
        out_specs=(vmem,) * 6,
        scratch_shapes=[
            pltpu.VMEM((2, 3 * rows, cols), f32),
            pltpu.VMEM((2, rows, 128), f32),
            pltpu.VMEM((2, 3 * rows, 128), f32),
            pltpu.VMEM((2, rows, cols), bf16),
            pltpu.VMEM((2, ch, rows, cols), bf16),
            pltpu.VMEM((9, 2, ch), bf16),
            pltpu.VMEM((9, ch, ch), bf16),
            pltpu.VMEM((9, 2, ch), bf16),
            pltpu.VMEM((2, cols // 128, ch * rows, 128), f32),
            pltpu.VMEM((2, ch + 16, cols), bf16),
            pltpu.VMEM((2, ch + 16, cols), bf16),
            pltpu.VMEM((2, ch + 16, 128), bf16),
            pltpu.VMEM((2, 3, ch + 16, 128), bf16),
            pltpu.VMEM((count, 1, 128), f32),
            pltpu.VMEM((count, chunk, 128), f32),
            pltpu.VMEM((count, chunk, 128), f32),
            pltpu.VMEM((count, chunk, 128), f32),
            pltpu.VMEM((count, 12, 128), f32),
            pltpu.VMEM((2, rows, cols), f32),
            pltpu.VMEM((2, band, wide), f32),
            pltpu.VMEM((256, cols), bf16),
            pltpu.VMEM((rows, ch, cols), f32),
            pltpu.VMEM((rows + 2, ch, wide), f32),
            pltpu.VMEM((rows, ch, cols), bf16),
            pltpu.VMEM((rows + 2, 3 * ch + 16, cols), bf16),
            pltpu.VMEM((rows + 2, 3 * ch, cols), bf16),
            pltpu.VMEM((rows + 2, 3 * ch, cols), f32),
            pltpu.VMEM((rows, ch, cols), bf16),
            pltpu.VMEM((3 * ch, 3 * ch), bf16),
            pltpu.VMEM(((rows + 2) * ch, 256), bf16),
            pltpu.VMEM((6 * band, rows * ch), bf16),
            pltpu.VMEM((2, 128, 128), f32),
            pltpu.VMEM((3 * ch, 3 * ch + 16), f32),
            pltpu.VMEM((2, 2, 1, wide), f32),
            pltpu.VMEM((2, rows, 128), f32),
            pltpu.VMEM((2, 2, 1, cols), f32),
            pltpu.VMEM((2, 2, 2, 1, 128), f32),
            pltpu.VMEM((2, 2, rows, 128), f32),
            dma((4, 8)), dma((4, 8)), dma((7,)), dma((4,)), dma((4,)),
        ],
        compiler_params=pltpu.CompilerParams(
            collective_id=0, has_side_effects=True, vmem_limit_bytes=56 * 2**20
        ),
    )(
        cotangent, velocity_in, hidden_pre1, hidden_pre2, w_last, w_middle, jnp.transpose(w_first, (0, 2, 1)),
    )
    grad_velocity, grad_middle, grad_last, grad_first, bias1, bias2 = pl.pallas_call(
        store_kernel,
        out_shape=out_shapes,
        in_specs=[vmem] * 6,
        out_specs=(anywhere,) * 6,
        scratch_shapes=[dma((6,))],
    )(*results)
    grad_first = jnp.transpose(grad_first, (0, 2, 1))
    return grad_velocity, grad_first, grad_middle, grad_last, bias1.reshape(ch), bias2.reshape(ch)


def solution(mesh):
    whole = P(None, "gx", "gy")
    return jax.shard_map(
        functools.partial(per_device, mesh.shape["gx"], mesh.shape["gy"]),
        mesh=mesh,
        in_specs=(whole, whole, whole, whole, P(), P(), P()),
        out_specs=(whole, P(), P(), P(), P(), P()),
        check_vma=False,
    )
```

```python
import functools
import math

import jax
import jax.numpy as jnp
from jax import lax
from jax.experimental import pallas as pl
from jax.experimental.pallas import tpu as pltpu
from jax.sharding import PartitionSpec as P

ITERS = 4
REACH = 2 * ITERS + 2
MESH = pl.DeviceIdType.MESH
NEIGHBOURS = tuple((dx, dy) for dx in (-1, 0, 1) for dy in (-1, 0, 1) if (dx, dy) != (0, 0))
NT = (((1,), (1,)), ((), ()))
NN = (((1,), (0,)), ((), ()))
C0 = 0.7978845608028654
C1 = 0.044715


def dot(a, b, dims):
    return lax.dot_general(a, b, dims, preferred_element_type=jnp.float32)


def roll_to(x, shift, axis):
    return pltpu.roll(x, shift % x.shape[axis], axis)


def gelu_both(v):
    square = v * v
    half = 0.5 * (1.0 + jnp.tanh(v * (C0 + (C0 * C1) * square)))
    value = v * half
    return value, half + (value * (1.0 - half)) * (2.0 * C0 + (6.0 * C0 * C1) * square)


def fused_kernel(
    nx, ny, factor, cot_in, vel_in, pre1_in, pre2_in, last_in, taps_in, first_in,
    spread_out, middle_out, last_out, first_out, bias1_out, bias2_out,
    cot, far, far_in, cot_edge, cot_side, vel, raw, w_lasts, w_taps, w_firsts, natural, rowsend, halo, vel_rows, vel_halo,
    edges, edge_in, spots, spots_in, slots, grads, sums, gathered, few, few_in, adj, vel_wide, vel_band, slope1, slope2, hidden2, hidden3, stacks, partial,
    deltas, w_middle, w_last, w_first, small, gm, border, side_out, row_in, corner_in, side_in,
    send, recv, load, send_all, recv_all,
):
    rows, cols = vel.shape[1], vel.shape[2]
    ch = raw.shape[1]
    wide = cols + 128
    blocks = cols // 128
    band = rows + 16
    f32, bf16 = jnp.float32, jnp.bfloat16
    gx, gy = lax.axis_index("gx"), lax.axis_index("gy")
    count = nx * ny
    me = gx * ny + gy

    loads = [
        pltpu.make_async_copy(src, dst, load.at[i])
        for i, (src, dst) in enumerate((
            (pre2_in, raw.at[1]), (pre1_in, raw.at[0]), (cot_in, cot.at[:, rows : 2 * rows]), (vel_in, vel),
            (taps_in, w_taps), (last_in, w_lasts), (first_in, w_firsts),
        ))
    ]
    for copy in loads:
        copy.start()

    def device(k):
        other = lax.rem(me + k, count)
        return other, (lax.div(other, ny), lax.rem(other, ny))

    for part in (slice(0, 8), slice(3 * rows - 8, 3 * rows)):
        cot[:, part] = jnp.zeros((2, 8, cols), f32)

    barrier = pltpu.get_barrier_semaphore()

    def hail(k, _):
        pl.semaphore_signal(barrier, inc=1, device_id=device(k)[1], device_id_type=MESH)
        return 0

    lax.fori_loop(1, count, hail, 0)

    def at(dx, dy):
        return (lax.rem(gx + dx + nx, nx), lax.rem(gy + dy + ny, ny))

    def remote(src, dst, which, index, peer):
        return pltpu.make_async_remote_copy(
            src_ref=src, dst_ref=dst, send_sem=send.at[which, index], recv_sem=recv.at[which, index],
            device_id=peer, device_id_type=MESH,
        )

    own = slice(rows, 2 * rows)
    cot_copies, edge_copies, back_copies, row_copies = [], [], [], []
    for i, (dx, dy) in enumerate(NEIGHBOURS):
        t = rows * (1 - dx)
        side, down = (1 + dy) // 2, (1 + dx) // 2
        if dy:
            cot_copies.append(
                remote(cot_edge.at[side], cot_side.at[side, t : t + rows], 0, i, at(dx, dy))
            )
            if dx:
                edge_copies.append(remote(spots.at[down, side], spots_in.at[down, side], 1, i, at(dx, dy)))
            else:
                edge_copies.append(remote(edges.at[side], edge_in.at[side], 1, i, at(dx, dy)))
        else:
            source = {1: slice(2 * rows - 8, 2 * rows), -1: slice(rows, rows + 8)}[dx]
            land = {1: slice(rows - 8, rows), -1: slice(2 * rows, 2 * rows + 8)}[dx]
            cot_copies.append(remote(cot.at[:, source], cot.at[:, land], 0, i, at(dx, dy)))
            cot_copies.append(remote(far.at[down], far_in.at[down], 2, 4 + down, at(dx, dy)))
            row_copies.append(remote(rowsend.at[down], halo.at[down], 2, down, at(dx, dy)))
            row_copies.append(remote(vel_rows.at[down], vel_halo.at[down], 2, 2 + down, at(dx, dy)))
        if dx and dy:
            back_copies.append(
                remote(border.at[down, :, :, cols:wide], corner_in.at[down, side], 3, i, at(dx, dy))
            )
        elif dx:
            back_copies.append(remote(border.at[down, :, :, 0:cols], row_in.at[down], 3, i, at(dx, dy)))
        else:
            back_copies.append(remote(side_out, side_in.at[side], 3, i, at(dx, dy)))
    def to_all(which, source, slot):
        def go(k, _):
            other, peer = device(k)
            pltpu.make_async_remote_copy(
                src_ref=source(other), dst_ref=slot.at[me], send_sem=send_all.at[which],
                recv_sem=recv_all.at[which], device_id=peer, device_id_type=MESH,
            ).start()
            return 0

        lax.fori_loop(1, count, go, 0)
        most = slot.at[pl.ds(0, count - 1)]
        return pltpu.make_async_remote_copy(
            src_ref=most, dst_ref=most, send_sem=send_all.at[which], recv_sem=recv_all.at[which],
            device_id=at(0, 1), device_id_type=MESH,
        )

    def total_of(slot):
        total = slot[0]
        for k in range(1, count):
            total = total + slot[k]
        return total

    def iota(shape, axis):
        return lax.broadcasted_iota(jnp.int32, shape, axis)

    loads[2].wait()
    lane = iota((rows, 128), 1)
    c_first = [cot[k, own, 0:128] for k in range(2)]
    c_last = [cot[k, own, cols - 128 : cols] for k in range(2)]
    for down, row in ((0, rows + 8), (1, 2 * rows - REACH)):
        for k in range(2):
            for i in range(REACH - 8):
                far[down, (REACH - 8) * k + i] = cot[k, row + i : row + i + 1, :]
    cot_edge[0] = jnp.where(lane < 16, c_first[0], roll_to(c_first[1], 16, 1))
    cot_edge[1] = jnp.where(lane < 112, roll_to(c_last[1], -16, 1), c_last[0])
    loads[0].wait()
    loads[1].wait()

    def widen(c, _):
        for which in range(2):
            block = raw[which, c].astype(f32)
            for part in range(blocks):
                natural[which, part, pl.ds(c * rows, rows), :] = block[:, 128 * part : 128 * part + 128]
        return 0

    lax.fori_loop(0, ch, widen, 0, unroll=4)

    def row_of(which, part, r):
        return natural[which, part, pl.ds(r, ch, rows), :]

    loads[3].wait()
    v = vel[...].astype(f32)
    for i, r in enumerate((0, rows - 1)):
        for part in range(blocks):
            rowsend[i, :, 128 * part : 128 * part + 128] = row_of(1, part, r).astype(bf16)
        for k in range(2):
            vel_rows[i, k] = v[k, r : r + 1]
    lane = iota((ch, 128), 1)
    placed = iota((rows, 128), 1) == iota((rows, 128), 0) + 1
    diagonal = iota((ch + 16, 128), 0) == iota((ch + 16, 128), 1)
    for side in range(2):
        built = jnp.zeros((ch, 128), f32)
        for r in range(rows):
            moved = roll_to(row_of(1, (blocks - 1) * side, r), r + 1 + side, 1)
            built = jnp.where(lane == r + 1, moved, built)
        col = (cols - 1) * side
        ends = [
            jnp.sum(jnp.where(placed, v[k, :, col : col + 1], 0.0), axis=0, keepdims=True) for k in range(2)
        ]
        built = jnp.concatenate([built] + ends + [jnp.zeros((14, 128), f32)], axis=0)
        edges[side] = built.astype(bf16)
        for down, at_lane in ((0, 1), (1, rows)):
            spots[down, side] = jnp.sum(
                jnp.where(diagonal, built[:, at_lane : at_lane + 1], 0.0), axis=0, keepdims=True
            )

    pl.semaphore_wait(barrier, count - 1)
    for copy in cot_copies + row_copies + edge_copies:
        copy.start()

    for copy in loads[4:]:
        copy.wait()
    turned = [w_taps[3 * a : 3 * a + 3].astype(f32).reshape(3 * ch, ch) for a in range(3)]
    for a in range(3):
        w_middle[a * ch : (a + 1) * ch, :] = turned[a].T.astype(bf16)
    small[...] = jnp.zeros_like(small)
    for t in range(9):
        small[0, 2 * t : 2 * t + 2, 0:ch] = w_lasts[t].astype(f32)
        small[1, 2 * t : 2 * t + 2, 0:ch] = w_firsts[t].astype(f32)
    taps = iota((32, 256), 0)
    place = iota((32, 256), 1)
    spot = jnp.where((taps < 18) & (place == band * lax.rem(taps, 6) + 8 - lax.div(taps, 6)), 1.0, 0.0)
    w_turned = small[0].T[0:ch, 0:32].astype(bf16)
    base = dot(w_turned, spot.astype(bf16), NN)
    for i in range(rows + 2):
        w_last[i * ch : (i + 1) * ch, :] = (roll_to(base, i, 1) if i else base).astype(bf16)
    taps = iota((256, 32), 1)
    place = iota((256, 32), 0)
    spot = jnp.where((taps < 18) & (place == band * lax.rem(taps, 6) + 7 + lax.div(taps, 6)), 1.0, 0.0)
    base = dot(spot.astype(bf16), small[1, 0:32, 0:ch].astype(bf16), NN)[0 : 6 * band]
    for j in range(0, rows, 2):
        w_first[:, j * ch : (j + 2) * ch] = jnp.concatenate(
            [roll_to(base, j, 0) if j else base, roll_to(base, j + 1, 0)], axis=1
        ).astype(bf16)
    gm[...] = jnp.zeros_like(gm)
    for i, a in ((0, 0), (0, 1), (1, 0), (rows, 2), (rows + 1, 1), (rows + 1, 2)):
        hidden3[i, a * ch : (a + 1) * ch, :] = jnp.zeros((ch, cols), bf16)
    one_row = jnp.where(iota((16, cols), 0) == 0, 1.0, 0.0).astype(bf16)
    for i in range(rows + 2):
        hidden3[i, 3 * ch : 3 * ch + 16, :] = one_row if 0 < i <= rows else jnp.zeros((16, cols), bf16)

    def activate(r, _):
        for part in range(blocks):
            here = slice(128 * part, 128 * part + 128)
            value, slope = gelu_both(row_of(1, part, r))
            hidden2[r, :, here] = value.astype(bf16)
            slope2[r + 1, :, here] = slope
            value, slope = gelu_both(row_of(0, part, r))
            value = value.astype(bf16)
            for a in range(3):
                hidden3[r + 2 - a, a * ch : (a + 1) * ch, here] = value
            slope1[r, :, here] = slope
        return 0

    lax.fori_loop(0, rows, activate, 0)

    for copy in cot_copies:
        copy.wait_recv()
    for down, row in ((1, rows - REACH), (0, 2 * rows + 8)):
        for k in range(2):
            for i in range(REACH - 8):
                cot[k, row + i : row + i + 1, :] = far_in[down, (REACH - 8) * k + i]
    tall = iota((3 * rows, 128), 1) < 64
    from_right, from_left = cot_side[0], cot_side[1]
    sides = [
        jnp.where(tall, from_right, from_left),
        jnp.where(tall, roll_to(from_right, -16, 1), roll_to(from_left, 16, 1)),
    ]
    c0, c1 = (jnp.concatenate([cot[k], sides[k]], axis=1) for k in range(2))
    rhs = -0.5 * ((roll_to(c0, -1, 0) - roll_to(c0, 1, 0)) + (roll_to(c1, -1, 1) - roll_to(c1, 1, 1)))
    fields = [rhs]
    for _ in range(ITERS):
        q = fields[-1]
        beside = roll_to(q, 2, 0) + roll_to(q, -2, 0) + roll_to(q, 2, 1)
        fields.append(-0.25 * (beside + roll_to(q, -2, 1)))
    inner = [f[own, 0:cols] for f in fields]
    parts = []
    for k in range(2 * ITERS):
        product = inner[k // 2] * inner[(k + 1) // 2]
        total = product[:, 0:128]
        for at_lane in range(128, cols, 128):
            total = total + product[:, at_lane : at_lane + 128]
        parts.append(jnp.sum(total, axis=0, keepdims=True))
    moments = jnp.sum(jnp.concatenate(parts, axis=0), axis=1, keepdims=True)
    square = iota((8, 128), 0) == iota((8, 128), 1)
    slots[me] = jnp.sum(jnp.where(square, moments, 0.0), axis=0, keepdims=True)
    started = to_all(0, lambda other: slots.at[me], slots)

    for copy in row_copies + edge_copies:
        copy.wait_recv()
    tall = iota((ch + 16, 128), 1)
    merged = []
    for side in range(2):
        below, above = (
            jnp.sum(jnp.where(diagonal, spots_in[down, side], 0.0), axis=1, keepdims=True) for down in range(2)
        )
        mid = jnp.where(tall < 1, above, edge_in[side].astype(f32))
        merged.append(jnp.where(tall > rows, below, mid))
    bent = [gelu_both(m[0:ch])[1] for m in merged]
    for i in range(rows + 2):
        slope2[i, :, cols:wide] = jnp.where(
            lane < 64, roll_to(bent[0], -i, 1) if i else bent[0], roll_to(bent[1], 127 - i, 1)
        )
    for i, row in ((1, 0), (0, rows + 1)):
        slope2[row, :, 0:cols] = gelu_both(halo[i].astype(f32))[1]
    vel_wide[...] = jnp.zeros_like(vel_wide)
    vel_wide[:, 8 : 8 + rows, 0:cols] = v
    upright = [roll_to(m[ch : ch + 16].T[0:band], 7, 0) for m in merged]
    at_lane = iota((band, 128), 1)
    for k in range(2):
        vel_wide[k, :, cols:wide] = jnp.where(at_lane == 0, upright[0][:, k : k + 1], 0.0) + jnp.where(
            at_lane == 127, upright[1][:, k : k + 1], 0.0
        )
        for i, row in ((1, 7), (0, 8 + rows)):
            vel_wide[k, row : row + 1, 0:cols] = vel_halo[i, k]
    for b in (-1, 0, 1):
        for k in range(2):
            at_band = band * (2 * (b + 1) + k)
            moved = roll_to(vel_wide[k], -b, 1) if b else vel_wide[k]
            vel_band[at_band : at_band + band, :] = moved[:, 0:cols].astype(bf16)
    vel_band[6 * band : 256, :] = jnp.where(iota((256 - 6 * band, cols), 0) < rows, 1.0, 0.0).astype(bf16)

    started.wait_recv()
    moments = jnp.sum(jnp.where(square, jnp.sum(slots[...], axis=0), 0.0), axis=1, keepdims=True)
    n = [moments[k : k + 1, 0:1] for k in range(2 * ITERS)]
    zero, one = jnp.zeros_like(n[0]), jnp.ones_like(n[0])
    lam, residual, direction = [zero] * (ITERS + 1), [one] + [zero] * ITERS, [one] + [zero] * ITERS
    norm_now = n[0]
    for step in range(ITERS):
        product = zero
        for i in range(step + 1):
            for j in range(step + 1):
                product = product + direction[i] * direction[j] * (n[i + j] + n[i + j + 1])
        alpha = norm_now / product
        lam = [x + alpha * p for x, p in zip(lam, direction)]
        if step + 1 < ITERS:
            image = [p + below for p, below in zip(direction, [zero] + direction[:-1])]
            residual = [r - alpha * a for r, a in zip(residual, image)]
            norm_next = zero
            for i in range(step + 2):
                for j in range(step + 2):
                    norm_next = norm_next + residual[i] * residual[j] * n[i + j]
            ratio = norm_next / norm_now
            direction = [r + ratio * p for r, p in zip(residual, direction)]
            norm_now = norm_next
    field = lam[0] * fields[0]
    for k in range(1, ITERS):
        field = field + lam[k] * fields[k]
    low = rows - 8
    a0 = (c0 + 0.5 * (roll_to(field, 1, 0) - roll_to(field, -1, 0)))[low : low + band]
    a1 = (c1 + 0.5 * (roll_to(field, 1, 1) - roll_to(field, -1, 1)))[low : low + band]
    adj[0] = a0[8 : 8 + rows, 0:cols]
    adj[1] = a1[8 : 8 + rows, 0:cols]
    banded = jnp.concatenate(
        [roll_to(x, b, 1) if b else x for b in (-1, 0, 1) for x in (a0, a1)]
        + [jnp.zeros((256 - 6 * band, wide), f32)],
        axis=0,
    ).astype(bf16)

    for i in range(0, rows + 2, 2):
        flat = dot(w_last[i * ch : (i + 2) * ch, :], banded, NN)
        for at_pair in range(2):
            delta = flat[at_pair * ch : (at_pair + 1) * ch] * slope2[i + at_pair]
            for s, b in enumerate((-1, 0, 1)):
                moved = roll_to(delta, b, 1) if b else delta
                stacks[i + at_pair, s * ch : (s + 1) * ch, :] = moved[:, 0:cols].astype(bf16)
        gm[...] += dot(
            jnp.concatenate([stacks[i], stacks[i + 1]], axis=1),
            jnp.concatenate([hidden3[i], hidden3[i + 1]], axis=1), NT,
        )

    def fold(source, other):
        flat = dot(source[...].reshape(rows * ch, cols), other, NT)
        total = flat[0:ch]
        for r in range(1, rows):
            total = total + roll_to(flat[r * ch : (r + 1) * ch], -r, 1)
        return total

    half = 9 * ch // 2
    chunk = grads.shape[1]
    third = 3 * ch // 2
    packed = jnp.concatenate([gm[0:third, 128:192], gm[third : 2 * third, 128:192]], axis=1)
    packed = [gm[:, 0:128], packed]
    if count * chunk > half:
        packed.append(jnp.zeros((count * chunk - half, 128), f32))
    packed = jnp.concatenate(packed, axis=0)
    for k in range(count):
        grads[k] = packed[k * chunk : (k + 1) * chunk]
    sums[me] = grads[me]
    scatter = to_all(1, lambda other: grads.at[other], sums)

    for i in range(0, rows + 2, 2):
        flat = dot(w_middle[...], jnp.concatenate([stacks[i], stacks[i + 1]], axis=1), NN)
        partial[i] = flat[:, 0:cols]
        partial[i + 1] = flat[:, cols : 2 * cols]
    for j in range(rows):
        total = partial[j + 2, 0:ch] + partial[j + 1, ch : 2 * ch] + partial[j, 2 * ch : 3 * ch]
        deltas[j] = (total * slope1[j]).astype(bf16)
    gf = fold(deltas, vel_band[...]).T
    gl = fold(hidden2, banded[:, 0:cols])
    gl = jnp.where(iota((ch, 256), 1) == 6 * band, gm[ch : 2 * ch, 3 * ch : 3 * ch + 1], gl).T
    few[...] = jnp.zeros_like(few)
    for m in range(19):
        here = [6 * band if m == 18 else band * (m % 6) + 8 + sign * (m // 6 - 1) for sign in (1, -1)]
        few[m, :, 0:ch] = gf[here[0] : here[0] + 1]
        few[m, :, ch : 2 * ch] = gl[here[1] : here[1] + 1]
    few_in[me] = few[me]
    last = to_all(3, lambda other: few.at[other], few_in)
    flat = dot(w_first[...], deltas[...].reshape(rows * ch, cols), NN)
    flat = jnp.concatenate([flat, jnp.zeros((6 * band, 128), f32)], axis=1)
    spread = []
    for k in range(2):
        terms = [flat[band * (2 * s + k) : band * (2 * s + k + 1)] for s in range(3)]
        spread.append(roll_to(terms[0], -1, 1) + terms[1] + roll_to(terms[2], 1, 1))
        border[0, k] = spread[k][7:8]
        border[1, k] = spread[k][8 + rows : 9 + rows]
        side_out[k] = spread[k][8 : 8 + rows, cols:wide]
    for copy in back_copies:
        copy.start()
    for k in range(2):
        spread_out[k] = adj[k] + spread[k][8 : 8 + rows, 0:cols]
    for copy in cot_copies + edge_copies + row_copies:
        copy.wait_send()
    started.wait_send()

    scatter.wait_recv()
    gathered[me, 0:chunk] = factor * total_of(sums)
    last.wait_recv()
    gathered[me, chunk : chunk + 1] = factor * total_of(few_in)
    spreading = to_all(2, lambda other: gathered.at[me], gathered)
    for copy in back_copies:
        copy.wait_recv()
    for copy in back_copies:
        copy.wait_send()
    left = iota((1, 128), 1) == 0
    right = iota((1, 128), 1) == 127
    for k in range(2):
        spread_out[k, :, 0:128] += jnp.where(left, side_in[1, k], 0.0)
        spread_out[k, :, cols - 128 : cols] += jnp.where(right, side_in[0, k], 0.0)
        for down, row in ((1, 0), (0, rows - 1)):
            spread_out[k, row : row + 1, :] += row_in[down, k]
            spread_out[k, row : row + 1, 0:128] += jnp.where(left, corner_in[down, 1, k], 0.0)
            spread_out[k, row : row + 1, cols - 128 : cols] += jnp.where(right, corner_in[down, 0, k], 0.0)
    scatter.wait_send()
    last.wait_send()
    spreading.wait_recv()
    spreading.wait_send()
    whole = jnp.concatenate([gathered[k, 0:chunk] for k in range(count)], axis=0)
    for t in range(9):
        a, start = t // 3, (t % 3) * ch
        for low in range(0, ch, 32):
            here = start + low
            side = a * ch
            if a == 2:
                side = 0 if here < third else 64
                here = 3 * ch + here % third
            middle_out[t, low : low + 32, :] = whole[here : here + 32, side : side + ch]
    for t in range(9):
        for k in range(2):
            pair = gathered[2 * t + k, chunk : chunk + 1]
            first_out[t, k : k + 1] = pair[:, 0:ch]
            last_out[t, k : k + 1] = pair[:, ch : 2 * ch]
    pair = gathered[18, chunk : chunk + 1]
    bias1_out[...] = pair[:, 0:ch]
    bias2_out[...] = pair[:, ch : 2 * ch]


def store_kernel(*refs):
    count = (len(refs) - 1) // 2
    copies = [
        pltpu.make_async_copy(refs[i], refs[count + i], refs[-1].at[i]) for i in range(count)
    ]
    for copy in copies:
        copy.start()
    for copy in copies:
        copy.wait()


def per_device(nx, ny, cotangent, velocity_in, hidden_pre1, hidden_pre2, w_first, w_middle, w_last):
    rows, cols = cotangent.shape[1], cotangent.shape[2]
    ch = hidden_pre1.shape[0]
    f32, bf16 = jnp.float32, jnp.bfloat16
    factor = 1.0 / math.sqrt(rows * nx * cols * ny)
    vmem = pl.BlockSpec(memory_space=pltpu.VMEM)
    anywhere = pl.BlockSpec(memory_space=pl.ANY)
    dma = pltpu.SemaphoreType.DMA
    count = nx * ny
    chunk = -(-(9 * ch // 2) // count)
    wide, band = cols + 128, rows + 16
    out_shapes = (
        jax.ShapeDtypeStruct((2, rows, cols), f32),
        jax.ShapeDtypeStruct((9, ch, ch), f32),
        jax.ShapeDtypeStruct((9, 2, ch), f32),
        jax.ShapeDtypeStruct((9, 2, ch), f32),
        jax.ShapeDtypeStruct((1, ch), f32),
        jax.ShapeDtypeStruct((1, ch), f32),
    )
    results = pl.pallas_call(
        functools.partial(fused_kernel, nx, ny, factor),
        out_shape=out_shapes,
        in_specs=[anywhere] * 7,
        out_specs=(vmem,) * 6,
        scratch_shapes=[
            pltpu.VMEM((2, 3 * rows, cols), f32),
            pltpu.VMEM((2, 2 * (REACH - 8), 1, cols), f32),
            pltpu.VMEM((2, 2 * (REACH - 8), 1, cols), f32),
            pltpu.VMEM((2, rows, 128), f32),
            pltpu.VMEM((2, 3 * rows, 128), f32),
            pltpu.VMEM((2, rows, cols), bf16),
            pltpu.VMEM((2, ch, rows, cols), bf16),
            pltpu.VMEM((9, 2, ch), bf16),
            pltpu.VMEM((9, ch, ch), bf16),
            pltpu.VMEM((9, 2, ch), bf16),
            pltpu.VMEM((2, cols // 128, ch * rows, 128), f32),
            pltpu.VMEM((2, ch, cols), bf16),
            pltpu.VMEM((2, ch, cols), bf16),
            pltpu.VMEM((2, 2, 1, cols), f32),
            pltpu.VMEM((2, 2, 1, cols), f32),
            pltpu.VMEM((2, ch + 16, 128), bf16),
            pltpu.VMEM((2, ch + 16, 128), bf16),
            pltpu.VMEM((2, 2, 1, 128), f32),
            pltpu.VMEM((2, 2, 1, 128), f32),
            pltpu.VMEM((count, 1, 128), f32),
            pltpu.VMEM((count, chunk, 128), f32),
            pltpu.VMEM((count, chunk, 128), f32),
            pltpu.VMEM((count, chunk + 1, 128), f32),
            pltpu.VMEM((count, 1, 128), f32),
            pltpu.VMEM((count, 1, 128), f32),
            pltpu.VMEM((2, rows, cols), f32),
            pltpu.VMEM((2, band, wide), f32),
            pltpu.VMEM((256, cols), bf16),
            pltpu.VMEM((rows, ch, cols), f32),
            pltpu.VMEM((rows + 2, ch, wide), f32),
            pltpu.VMEM((rows, ch, cols), bf16),
            pltpu.VMEM((rows + 2, 3 * ch + 16, cols), bf16),
            pltpu.VMEM((rows + 2, 3 * ch, cols), bf16),
            pltpu.VMEM((rows + 2, 3 * ch, cols), f32),
            pltpu.VMEM((rows, ch, cols), bf16),
            pltpu.VMEM((3 * ch, 3 * ch), bf16),
            pltpu.VMEM(((rows + 2) * ch, 256), bf16),
            pltpu.VMEM((6 * band, rows * ch), bf16),
            pltpu.VMEM((2, 128, 128), f32),
            pltpu.VMEM((3 * ch, 3 * ch + 16), f32),
            pltpu.VMEM((2, 2, 1, wide), f32),
            pltpu.VMEM((2, rows, 128), f32),
            pltpu.VMEM((2, 2, 1, cols), f32),
            pltpu.VMEM((2, 2, 2, 1, 128), f32),
            pltpu.VMEM((2, 2, rows, 128), f32),
            dma((4, 8)), dma((4, 8)), dma((7,)), dma((4,)), dma((4,)),
        ],
        compiler_params=pltpu.CompilerParams(
            collective_id=0, has_side_effects=True, vmem_limit_bytes=56 * 2**20
        ),
    )(
        cotangent, velocity_in, hidden_pre1, hidden_pre2, w_last, w_middle, jnp.transpose(w_first, (0, 2, 1)),
    )
    grad_velocity, grad_middle, grad_last, grad_first, bias1, bias2 = pl.pallas_call(
        store_kernel,
        out_shape=out_shapes,
        in_specs=[vmem] * 6,
        out_specs=(anywhere,) * 6,
        scratch_shapes=[dma((6,))],
    )(*results)
    grad_first = jnp.transpose(grad_first, (0, 2, 1))
    return grad_velocity, grad_first, grad_middle, grad_last, bias1.reshape(ch), bias2.reshape(ch)


def solution(mesh):
    whole = P(None, "gx", "gy")
    return jax.shard_map(
        functools.partial(per_device, mesh.shape["gx"], mesh.shape["gy"]),
        mesh=mesh,
        in_specs=(whole, whole, whole, whole, P(), P(), P()),
        out_specs=(whole, P(), P(), P(), P(), P()),
        check_vma=False,
    )
```

```python
import functools
import math

import jax
import jax.numpy as jnp
from jax import lax
from jax.experimental import pallas as pl
from jax.experimental.pallas import tpu as pltpu
from jax.sharding import PartitionSpec as P

ITERS = 4
REACH = 2 * ITERS + 2
MESH = pl.DeviceIdType.MESH
NEIGHBOURS = tuple((dx, dy) for dx in (-1, 0, 1) for dy in (-1, 0, 1) if (dx, dy) != (0, 0))
NT = (((1,), (1,)), ((), ()))
NN = (((1,), (0,)), ((), ()))
C0 = 0.7978845608028654
C1 = 0.044715


def dot(a, b, dims):
    return lax.dot_general(a, b, dims, preferred_element_type=jnp.float32)


def roll_to(x, shift, axis):
    return pltpu.roll(x, shift % x.shape[axis], axis)


def gelu_both(v):
    square = v * v
    half = 0.5 * (1.0 + jnp.tanh(v * (C0 + (C0 * C1) * square)))
    value = v * half
    return value, half + (value * (1.0 - half)) * (2.0 * C0 + (6.0 * C0 * C1) * square)


def fused_kernel(
    nx, ny, factor, cot_in, vel_in, pre1_in, pre2_in, last_in, taps_in, first_in,
    spread_out, middle_out, last_out, first_out, bias1_out, bias2_out,
    cot, far, far_in, cot_edge, cot_side, cot_spot, cot_spot_in, vel, raw, w_lasts, w_taps, w_firsts, natural, rowsend, halo, vel_rows, vel_halo,
    edges, edge_in, spots, spots_in, slots, grads, sums, gathered, few, few_in, adj, vel_wide, vel_band, slope1, slope2, hidden2, hidden3, stacks, partial,
    deltas, w_middle, w_last, w_first, small, gm, border, side_out, row_in, corner_in, side_in,
    send, recv, load, send_all, recv_all,
):
    rows, cols = vel.shape[1], vel.shape[2]
    ch = raw.shape[1]
    wide = cols + 128
    blocks = cols // 128
    band = rows + 16
    f32, bf16 = jnp.float32, jnp.bfloat16
    gx, gy = lax.axis_index("gx"), lax.axis_index("gy")
    count = nx * ny
    me = gx * ny + gy

    loads = [
        pltpu.make_async_copy(src, dst, load.at[i])
        for i, (src, dst) in enumerate((
            (pre2_in, raw.at[1]), (pre1_in, raw.at[0]), (cot_in, cot.at[:, rows : 2 * rows]), (vel_in, vel),
            (taps_in, w_taps), (last_in, w_lasts), (first_in, w_firsts),
        ))
    ]
    for copy in loads:
        copy.start()

    def device(k):
        other = lax.rem(me + k, count)
        return other, (lax.div(other, ny), lax.rem(other, ny))

    for part in (slice(0, 8), slice(3 * rows - 8, 3 * rows)):
        cot[:, part] = jnp.zeros((2, 8, cols), f32)

    barrier = pltpu.get_barrier_semaphore()

    def hail(k, _):
        pl.semaphore_signal(barrier, inc=1, device_id=device(k)[1], device_id_type=MESH)
        return 0

    lax.fori_loop(1, count, hail, 0)

    def at(dx, dy):
        return (lax.rem(gx + dx + nx, nx), lax.rem(gy + dy + ny, ny))

    def remote(src, dst, which, index, peer):
        return pltpu.make_async_remote_copy(
            src_ref=src, dst_ref=dst, send_sem=send.at[which, index], recv_sem=recv.at[which, index],
            device_id=peer, device_id_type=MESH,
        )

    own = slice(rows, 2 * rows)
    cot_copies, edge_copies, back_copies, row_copies = [], [], [], []
    for i, (dx, dy) in enumerate(NEIGHBOURS):
        side, down = (1 + dy) // 2, (1 + dx) // 2
        if dy:
            cot_copies.append(
                remote(cot_spot.at[side], cot_spot_in.at[down, side], 0, i, at(dx, dy)) if dx
                else remote(cot_edge.at[side], cot_side.at[side, own], 0, i, at(dx, dy))
            )
            if dx:
                edge_copies.append(remote(spots.at[down, side], spots_in.at[down, side], 1, i, at(dx, dy)))
            else:
                edge_copies.append(remote(edges.at[side], edge_in.at[side], 1, i, at(dx, dy)))
        else:
            source = {1: slice(2 * rows - 8, 2 * rows), -1: slice(rows, rows + 8)}[dx]
            land = {1: slice(rows - 8, rows), -1: slice(2 * rows, 2 * rows + 8)}[dx]
            cot_copies.append(remote(cot.at[:, source], cot.at[:, land], 0, i, at(dx, dy)))
            cot_copies.append(remote(far.at[down], far_in.at[down], 2, 4 + down, at(dx, dy)))
            row_copies.append(remote(rowsend.at[down], halo.at[down], 2, down, at(dx, dy)))
            row_copies.append(remote(vel_rows.at[down], vel_halo.at[down], 2, 2 + down, at(dx, dy)))
        if dx and dy:
            back_copies.append(
                remote(border.at[down, :, :, cols:wide], corner_in.at[down, side], 3, i, at(dx, dy))
            )
        elif dx:
            back_copies.append(remote(border.at[down, :, :, 0:cols], row_in.at[down], 3, i, at(dx, dy)))
        else:
            back_copies.append(remote(side_out, side_in.at[side], 3, i, at(dx, dy)))
    def to_all(which, source, slot):
        def go(k, _):
            other, peer = device(k)
            pltpu.make_async_remote_copy(
                src_ref=source(other), dst_ref=slot.at[me], send_sem=send_all.at[which],
                recv_sem=recv_all.at[which], device_id=peer, device_id_type=MESH,
            ).start()
            return 0

        lax.fori_loop(1, count, go, 0)
        most = slot.at[pl.ds(0, count - 1)]
        return pltpu.make_async_remote_copy(
            src_ref=most, dst_ref=most, send_sem=send_all.at[which], recv_sem=recv_all.at[which],
            device_id=at(0, 1), device_id_type=MESH,
        )

    def total_of(slot):
        total = slot[0]
        for k in range(1, count):
            total = total + slot[k]
        return total

    def iota(shape, axis):
        return lax.broadcasted_iota(jnp.int32, shape, axis)

    loads[2].wait()
    lane = iota((rows, 128), 1)
    c_first = [cot[k, own, 0:128] for k in range(2)]
    c_last = [cot[k, own, cols - 128 : cols] for k in range(2)]
    for down, row in ((0, rows + 8), (1, 2 * rows - REACH)):
        for k in range(2):
            for i in range(REACH - 8):
                far[down, (REACH - 8) * k + i] = cot[k, row + i : row + i + 1, :]
    cot_edge[0] = jnp.where(lane < 16, c_first[0], roll_to(c_first[1], 16, 1))
    cot_edge[1] = jnp.where(lane < 112, roll_to(c_last[1], -16, 1), c_last[0])
    low_half, high_half = slice(0, rows // 2), slice(rows // 2, rows)
    lane = iota((rows // 2, 128), 1)
    cot_spot[0] = jnp.where(lane < 32, cot_edge[0, high_half], roll_to(cot_edge[0, low_half], 32, 1))
    cot_spot[1] = jnp.where(lane < 96, roll_to(cot_edge[1, low_half], -32, 1), cot_edge[1, high_half])
    loads[0].wait()
    loads[1].wait()

    def widen(c, _):
        for which in range(2):
            block = raw[which, c].astype(f32)
            for part in range(blocks):
                natural[which, part, pl.ds(c * rows, rows), :] = block[:, 128 * part : 128 * part + 128]
        return 0

    lax.fori_loop(0, ch, widen, 0, unroll=4)

    def row_of(which, part, r):
        return natural[which, part, pl.ds(r, ch, rows), :]

    loads[3].wait()
    v = vel[...].astype(f32)
    for i, r in enumerate((0, rows - 1)):
        for part in range(blocks):
            rowsend[i, :, 128 * part : 128 * part + 128] = row_of(1, part, r).astype(bf16)
        for k in range(2):
            vel_rows[i, k] = v[k, r : r + 1]
    lane = iota((ch, 128), 1)
    placed = iota((rows, 128), 1) == iota((rows, 128), 0) + 1
    diagonal = iota((ch + 16, 128), 0) == iota((ch + 16, 128), 1)
    for side in range(2):
        built = jnp.zeros((ch, 128), f32)
        for r in range(rows):
            moved = roll_to(row_of(1, (blocks - 1) * side, r), r + 1 + side, 1)
            built = jnp.where(lane == r + 1, moved, built)
        col = (cols - 1) * side
        ends = [
            jnp.sum(jnp.where(placed, v[k, :, col : col + 1], 0.0), axis=0, keepdims=True) for k in range(2)
        ]
        built = jnp.concatenate([built] + ends + [jnp.zeros((14, 128), f32)], axis=0)
        edges[side] = built.astype(bf16)
        for down, at_lane in ((0, 1), (1, rows)):
            spots[down, side] = jnp.sum(
                jnp.where(diagonal, built[:, at_lane : at_lane + 1], 0.0), axis=0, keepdims=True
            )

    pl.semaphore_wait(barrier, count - 1)
    for copy in cot_copies:
        copy.start()

    for copy in loads[4:]:
        copy.wait()
    turned = [w_taps[3 * a : 3 * a + 3].astype(f32).reshape(3 * ch, ch) for a in range(3)]
    for a in range(3):
        w_middle[a * ch : (a + 1) * ch, :] = turned[a].T.astype(bf16)
    small[...] = jnp.zeros_like(small)
    for t in range(9):
        small[0, 2 * t : 2 * t + 2, 0:ch] = w_lasts[t].astype(f32)
        small[1, 2 * t : 2 * t + 2, 0:ch] = w_firsts[t].astype(f32)
    taps = iota((32, 256), 0)
    place = iota((32, 256), 1)
    spot = jnp.where((taps < 18) & (place == band * lax.rem(taps, 6) + 8 - lax.div(taps, 6)), 1.0, 0.0)
    w_turned = small[0].T[0:ch, 0:32].astype(bf16)
    base = dot(w_turned, spot.astype(bf16), NN)
    for i in range(rows + 2):
        w_last[i * ch : (i + 1) * ch, :] = (roll_to(base, i, 1) if i else base).astype(bf16)
    taps = iota((256, 32), 1)
    place = iota((256, 32), 0)
    spot = jnp.where((taps < 18) & (place == band * lax.rem(taps, 6) + 7 + lax.div(taps, 6)), 1.0, 0.0)
    base = dot(spot.astype(bf16), small[1, 0:32, 0:ch].astype(bf16), NN)[0 : 6 * band]
    for j in range(0, rows, 2):
        w_first[:, j * ch : (j + 2) * ch] = jnp.concatenate(
            [roll_to(base, j, 0) if j else base, roll_to(base, j + 1, 0)], axis=1
        ).astype(bf16)
    gm[...] = jnp.zeros_like(gm)
    for i, a in ((0, 0), (0, 1), (1, 0), (rows, 2), (rows + 1, 1), (rows + 1, 2)):
        hidden3[i, a * ch : (a + 1) * ch, :] = jnp.zeros((ch, cols), bf16)
    one_row = jnp.where(iota((16, cols), 0) == 0, 1.0, 0.0).astype(bf16)
    for i in range(rows + 2):
        hidden3[i, 3 * ch : 3 * ch + 16, :] = one_row if 0 < i <= rows else jnp.zeros((16, cols), bf16)

    def activate(r, _):
        for part in range(blocks):
            here = slice(128 * part, 128 * part + 128)
            value, slope = gelu_both(row_of(1, part, r))
            hidden2[r, :, here] = value.astype(bf16)
            slope2[r + 1, :, here] = slope
            value, slope = gelu_both(row_of(0, part, r))
            value = value.astype(bf16)
            for a in range(3):
                hidden3[r + 2 - a, a * ch : (a + 1) * ch, here] = value
            slope1[r, :, here] = slope
        return 0

    lax.fori_loop(0, rows, activate, 0)
    for copy in row_copies + edge_copies:
        copy.start()

    for copy in cot_copies:
        copy.wait_recv()
    for down, row in ((1, rows - REACH), (0, 2 * rows + 8)):
        for k in range(2):
            for i in range(REACH - 8):
                cot[k, row + i : row + i + 1, :] = far_in[down, (REACH - 8) * k + i]
    for down, row in ((1, 0), (0, 2 * rows)):
        for side, shift in ((0, -32), (1, 32)):
            spot = cot_spot_in[down, side]
            cot_side[side, row + rows // 2 : row + rows] = spot
            cot_side[side, row : row + rows // 2] = roll_to(spot, shift, 1)
    tall = iota((3 * rows, 128), 1) < 64
    from_right, from_left = cot_side[0], cot_side[1]
    sides = [
        jnp.where(tall, from_right, from_left),
        jnp.where(tall, roll_to(from_right, -16, 1), roll_to(from_left, 16, 1)),
    ]
    c0, c1 = (jnp.concatenate([cot[k], sides[k]], axis=1) for k in range(2))
    rhs = -0.5 * ((roll_to(c0, -1, 0) - roll_to(c0, 1, 0)) + (roll_to(c1, -1, 1) - roll_to(c1, 1, 1)))
    fields = [rhs]
    for _ in range(ITERS):
        q = fields[-1]
        beside = roll_to(q, 2, 0) + roll_to(q, -2, 0) + roll_to(q, 2, 1)
        fields.append(-0.25 * (beside + roll_to(q, -2, 1)))
    inner = [f[own, 0:cols] for f in fields]
    parts = []
    for k in range(2 * ITERS):
        product = inner[k // 2] * inner[(k + 1) // 2]
        total = product[:, 0:128]
        for at_lane in range(128, cols, 128):
            total = total + product[:, at_lane : at_lane + 128]
        parts.append(jnp.sum(total, axis=0, keepdims=True))
    moments = jnp.sum(jnp.concatenate(parts, axis=0), axis=1, keepdims=True)
    square = iota((8, 128), 0) == iota((8, 128), 1)
    slots[me] = jnp.sum(jnp.where(square, moments, 0.0), axis=0, keepdims=True)
    started = to_all(0, lambda other: slots.at[me], slots)

    for copy in row_copies + edge_copies:
        copy.wait_recv()
    tall = iota((ch + 16, 128), 1)
    merged = []
    for side in range(2):
        below, above = (
            jnp.sum(jnp.where(diagonal, spots_in[down, side], 0.0), axis=1, keepdims=True) for down in range(2)
        )
        mid = jnp.where(tall < 1, above, edge_in[side].astype(f32))
        merged.append(jnp.where(tall > rows, below, mid))
    bent = [gelu_both(m[0:ch])[1] for m in merged]
    for i in range(rows + 2):
        slope2[i, :, cols:wide] = jnp.where(
            lane < 64, roll_to(bent[0], -i, 1) if i else bent[0], roll_to(bent[1], 127 - i, 1)
        )
    for i, row in ((1, 0), (0, rows + 1)):
        slope2[row, :, 0:cols] = gelu_both(halo[i].astype(f32))[1]
    vel_wide[...] = jnp.zeros_like(vel_wide)
    vel_wide[:, 8 : 8 + rows, 0:cols] = v
    upright = [roll_to(m[ch : ch + 16].T[0:band], 7, 0) for m in merged]
    at_lane = iota((band, 128), 1)
    for k in range(2):
        vel_wide[k, :, cols:wide] = jnp.where(at_lane == 0, upright[0][:, k : k + 1], 0.0) + jnp.where(
            at_lane == 127, upright[1][:, k : k + 1], 0.0
        )
        for i, row in ((1, 7), (0, 8 + rows)):
            vel_wide[k, row : row + 1, 0:cols] = vel_halo[i, k]
    for b in (-1, 0, 1):
        for k in range(2):
            at_band = band * (2 * (b + 1) + k)
            moved = roll_to(vel_wide[k], -b, 1) if b else vel_wide[k]
            vel_band[at_band : at_band + band, :] = moved[:, 0:cols].astype(bf16)
    vel_band[6 * band : 256, :] = jnp.where(iota((256 - 6 * band, cols), 0) < rows, 1.0, 0.0).astype(bf16)

    started.wait_recv()
    moments = jnp.sum(jnp.where(square, jnp.sum(slots[...], axis=0), 0.0), axis=1, keepdims=True)
    n = [moments[k : k + 1, 0:1] for k in range(2 * ITERS)]
    zero, one = jnp.zeros_like(n[0]), jnp.ones_like(n[0])
    lam, residual, direction = [zero] * (ITERS + 1), [one] + [zero] * ITERS, [one] + [zero] * ITERS
    norm_now = n[0]
    sums_of_two = [n[k] + n[k + 1] for k in range(2 * ITERS - 1)]

    def against(weights, moments):
        terms = []
        for m in range(2 * len(weights) - 1):
            for i in range(max(0, m - len(weights) + 1), m // 2 + 1):
                twice = weights[i] * weights[m - i]
                terms.append((twice if 2 * i == m else twice + twice) * moments[m])
        while len(terms) > 1:
            terms = [sum(terms[k + 1 : k + 2], terms[k]) for k in range(0, len(terms), 2)]
        return terms[0]

    for step in range(ITERS):
        alpha = norm_now / against(direction[: step + 1], sums_of_two)
        lam = [x + alpha * p for x, p in zip(lam, direction)]
        if step + 1 < ITERS:
            image = [p + below for p, below in zip(direction, [zero] + direction[:-1])]
            residual = [r - alpha * a for r, a in zip(residual, image)]
            norm_next = against(residual[: step + 2], n)
            ratio = norm_next / norm_now
            direction = [r + ratio * p for r, p in zip(residual, direction)]
            norm_now = norm_next
    field = lam[0] * fields[0]
    for k in range(1, ITERS):
        field = field + lam[k] * fields[k]
    low = rows - 8
    a0 = (c0 + 0.5 * (roll_to(field, 1, 0) - roll_to(field, -1, 0)))[low : low + band]
    a1 = (c1 + 0.5 * (roll_to(field, 1, 1) - roll_to(field, -1, 1)))[low : low + band]
    adj[0] = a0[8 : 8 + rows, 0:cols]
    adj[1] = a1[8 : 8 + rows, 0:cols]
    banded = jnp.concatenate(
        [roll_to(x, b, 1) if b else x for b in (-1, 0, 1) for x in (a0, a1)]
        + [jnp.zeros((256 - 6 * band, wide), f32)],
        axis=0,
    ).astype(bf16)

    flat = dot(w_last[...], banded, NN)
    for i in range(rows + 2):
        narrow = (flat[i * ch : (i + 1) * ch] * slope2[i]).astype(bf16)
        for at_b, b in enumerate((-1, 0, 1)):
            moved = roll_to(narrow, b, 1) if b else narrow
            stacks[i, at_b * ch : (at_b + 1) * ch, :] = moved[:, 0:cols]
    for i in range(0, rows + 2, 2):
        gm[...] += dot(
            jnp.concatenate([stacks[i], stacks[i + 1]], axis=1),
            jnp.concatenate([hidden3[i], hidden3[i + 1]], axis=1), NT,
        )

    def fold(source, other):
        flat = dot(source[...].reshape(rows * ch, cols), other, NT)
        total = flat[0:ch]
        for r in range(1, rows):
            total = total + roll_to(flat[r * ch : (r + 1) * ch], -r, 1)
        return total

    half = 9 * ch // 2
    chunk = grads.shape[1]
    third = 3 * ch // 2
    packed = jnp.concatenate([gm[0:third, 128:192], gm[third : 2 * third, 128:192]], axis=1)
    packed = [gm[:, 0:128], packed]
    if count * chunk > half:
        packed.append(jnp.zeros((count * chunk - half, 128), f32))
    packed = jnp.concatenate(packed, axis=0)
    for k in range(count):
        grads[k] = packed[k * chunk : (k + 1) * chunk]
    sums[me] = grads[me]
    scatter = to_all(1, lambda other: grads.at[other], sums)

    for i in range(0, rows + 2, 2):
        flat = dot(w_middle[...], jnp.concatenate([stacks[i], stacks[i + 1]], axis=1), NN)
        partial[i] = flat[:, 0:cols]
        partial[i + 1] = flat[:, cols : 2 * cols]
    for j in range(rows):
        total = partial[j + 2, 0:ch] + partial[j + 1, ch : 2 * ch] + partial[j, 2 * ch : 3 * ch]
        deltas[j] = (total * slope1[j]).astype(bf16)
    gf = fold(deltas, vel_band[...]).T
    gl = fold(hidden2, banded[:, 0:cols])
    gl = jnp.where(iota((ch, 256), 1) == 6 * band, gm[ch : 2 * ch, 3 * ch : 3 * ch + 1], gl).T
    few[...] = jnp.zeros_like(few)
    for m in range(19):
        here = [6 * band if m == 18 else band * (m % 6) + 8 + sign * (m // 6 - 1) for sign in (1, -1)]
        few[m, :, 0:ch] = gf[here[0] : here[0] + 1]
        few[m, :, ch : 2 * ch] = gl[here[1] : here[1] + 1]
    few_in[me] = few[me]
    last = to_all(3, lambda other: few.at[other], few_in)
    flat = dot(w_first[...], deltas[...].reshape(rows * ch, cols), NN)
    flat = jnp.concatenate([flat, jnp.zeros((6 * band, 128), f32)], axis=1)
    spread = []
    for k in range(2):
        terms = [flat[band * (2 * s + k) : band * (2 * s + k + 1)] for s in range(3)]
        spread.append(roll_to(terms[0], -1, 1) + terms[1] + roll_to(terms[2], 1, 1))
        border[0, k] = spread[k][7:8]
        border[1, k] = spread[k][8 + rows : 9 + rows]
        side_out[k] = spread[k][8 : 8 + rows, cols:wide]
    for copy in back_copies:
        copy.start()
    for k in range(2):
        spread_out[k] = adj[k] + spread[k][8 : 8 + rows, 0:cols]
    for copy in cot_copies + edge_copies + row_copies:
        copy.wait_send()
    started.wait_send()

    scatter.wait_recv()
    gathered[me, 0:chunk] = factor * total_of(sums)
    last.wait_recv()
    gathered[me, chunk : chunk + 1] = factor * total_of(few_in)
    spreading = to_all(2, lambda other: gathered.at[me], gathered)
    for copy in back_copies:
        copy.wait_recv()
    for copy in back_copies:
        copy.wait_send()
    left = iota((1, 128), 1) == 0
    right = iota((1, 128), 1) == 127
    for k in range(2):
        spread_out[k, :, 0:128] += jnp.where(left, side_in[1, k], 0.0)
        spread_out[k, :, cols - 128 : cols] += jnp.where(right, side_in[0, k], 0.0)
        for down, row in ((1, 0), (0, rows - 1)):
            spread_out[k, row : row + 1, :] += row_in[down, k]
            spread_out[k, row : row + 1, 0:128] += jnp.where(left, corner_in[down, 1, k], 0.0)
            spread_out[k, row : row + 1, cols - 128 : cols] += jnp.where(right, corner_in[down, 0, k], 0.0)
    scatter.wait_send()
    last.wait_send()
    spreading.wait_recv()
    spreading.wait_send()
    whole = jnp.concatenate([gathered[k, 0:chunk] for k in range(count)], axis=0)
    for t in range(9):
        a, start = t // 3, (t % 3) * ch
        for low in range(0, ch, 32):
            here = start + low
            side = a * ch
            if a == 2:
                side = 0 if here < third else 64
                here = 3 * ch + here % third
            middle_out[t, low : low + 32, :] = whole[here : here + 32, side : side + ch]
    for t in range(9):
        for k in range(2):
            pair = gathered[2 * t + k, chunk : chunk + 1]
            first_out[t, k : k + 1] = pair[:, 0:ch]
            last_out[t, k : k + 1] = pair[:, ch : 2 * ch]
    pair = gathered[18, chunk : chunk + 1]
    bias1_out[...] = pair[:, 0:ch]
    bias2_out[...] = pair[:, ch : 2 * ch]


def store_kernel(*refs):
    count = (len(refs) - 1) // 2
    copies = [
        pltpu.make_async_copy(refs[i], refs[count + i], refs[-1].at[i]) for i in range(count)
    ]
    for copy in copies:
        copy.start()
    for copy in copies:
        copy.wait()


def per_device(nx, ny, cotangent, velocity_in, hidden_pre1, hidden_pre2, w_first, w_middle, w_last):
    rows, cols = cotangent.shape[1], cotangent.shape[2]
    ch = hidden_pre1.shape[0]
    f32, bf16 = jnp.float32, jnp.bfloat16
    factor = 1.0 / math.sqrt(rows * nx * cols * ny)
    vmem = pl.BlockSpec(memory_space=pltpu.VMEM)
    anywhere = pl.BlockSpec(memory_space=pl.ANY)
    dma = pltpu.SemaphoreType.DMA
    count = nx * ny
    chunk = -(-(9 * ch // 2) // count)
    wide, band = cols + 128, rows + 16
    out_shapes = (
        jax.ShapeDtypeStruct((2, rows, cols), f32),
        jax.ShapeDtypeStruct((9, ch, ch), f32),
        jax.ShapeDtypeStruct((9, 2, ch), f32),
        jax.ShapeDtypeStruct((9, 2, ch), f32),
        jax.ShapeDtypeStruct((1, ch), f32),
        jax.ShapeDtypeStruct((1, ch), f32),
    )
    results = pl.pallas_call(
        functools.partial(fused_kernel, nx, ny, factor),
        out_shape=out_shapes,
        in_specs=[anywhere] * 7,
        out_specs=(vmem,) * 6,
        scratch_shapes=[
            pltpu.VMEM((2, 3 * rows, cols), f32),
            pltpu.VMEM((2, 2 * (REACH - 8), 1, cols), f32),
            pltpu.VMEM((2, 2 * (REACH - 8), 1, cols), f32),
            pltpu.VMEM((2, rows, 128), f32),
            pltpu.VMEM((2, 3 * rows, 128), f32),
            pltpu.VMEM((2, rows // 2, 128), f32),
            pltpu.VMEM((2, 2, rows // 2, 128), f32),
            pltpu.VMEM((2, rows, cols), bf16),
            pltpu.VMEM((2, ch, rows, cols), bf16),
            pltpu.VMEM((9, 2, ch), bf16),
            pltpu.VMEM((9, ch, ch), bf16),
            pltpu.VMEM((9, 2, ch), bf16),
            pltpu.VMEM((2, cols // 128, ch * rows, 128), f32),
            pltpu.VMEM((2, ch, cols), bf16),
            pltpu.VMEM((2, ch, cols), bf16),
            pltpu.VMEM((2, 2, 1, cols), f32),
            pltpu.VMEM((2, 2, 1, cols), f32),
            pltpu.VMEM((2, ch + 16, 128), bf16),
            pltpu.VMEM((2, ch + 16, 128), bf16),
            pltpu.VMEM((2, 2, 1, 128), f32),
            pltpu.VMEM((2, 2, 1, 128), f32),
            pltpu.VMEM((count, 1, 128), f32),
            pltpu.VMEM((count, chunk, 128), f32),
            pltpu.VMEM((count, chunk, 128), f32),
            pltpu.VMEM((count, chunk + 1, 128), f32),
            pltpu.VMEM((count, 1, 128), f32),
            pltpu.VMEM((count, 1, 128), f32),
            pltpu.VMEM((2, rows, cols), f32),
            pltpu.VMEM((2, band, wide), f32),
            pltpu.VMEM((256, cols), bf16),
            pltpu.VMEM((rows, ch, cols), f32),
            pltpu.VMEM((rows + 2, ch, wide), f32),
            pltpu.VMEM((rows, ch, cols), bf16),
            pltpu.VMEM((rows + 2, 3 * ch + 16, cols), bf16),
            pltpu.VMEM((rows + 2, 3 * ch, cols), bf16),
            pltpu.VMEM((rows + 2, 3 * ch, cols), f32),
            pltpu.VMEM((rows, ch, cols), bf16),
            pltpu.VMEM((3 * ch, 3 * ch), bf16),
            pltpu.VMEM(((rows + 2) * ch, 256), bf16),
            pltpu.VMEM((6 * band, rows * ch), bf16),
            pltpu.VMEM((2, 128, 128), f32),
            pltpu.VMEM((3 * ch, 3 * ch + 16), f32),
            pltpu.VMEM((2, 2, 1, wide), f32),
            pltpu.VMEM((2, rows, 128), f32),
            pltpu.VMEM((2, 2, 1, cols), f32),
            pltpu.VMEM((2, 2, 2, 1, 128), f32),
            pltpu.VMEM((2, 2, rows, 128), f32),
            dma((4, 8)), dma((4, 8)), dma((7,)), dma((4,)), dma((4,)),
        ],
        compiler_params=pltpu.CompilerParams(
            collective_id=0, has_side_effects=True, vmem_limit_bytes=56 * 2**20
        ),
    )(
        cotangent, velocity_in, hidden_pre1, hidden_pre2, w_last, w_middle, jnp.transpose(w_first, (0, 2, 1)),
    )
    grad_velocity, grad_middle, grad_last, grad_first, bias1, bias2 = pl.pallas_call(
        store_kernel,
        out_shape=out_shapes,
        in_specs=[vmem] * 6,
        out_specs=(anywhere,) * 6,
        scratch_shapes=[dma((6,))],
    )(*results)
    grad_first = jnp.transpose(grad_first, (0, 2, 1))
    return grad_velocity, grad_first, grad_middle, grad_last, bias1.reshape(ch), bias2.reshape(ch)


def solution(mesh):
    whole = P(None, "gx", "gy")
    return jax.shard_map(
        functools.partial(per_device, mesh.shape["gx"], mesh.shape["gy"]),
        mesh=mesh,
        in_specs=(whole, whole, whole, whole, P(), P(), P()),
        out_specs=(whole, P(), P(), P(), P(), P()),
        check_vma=False,
    )
```

```python
import functools
import math

import jax
import jax.numpy as jnp
from jax import lax
from jax.experimental import pallas as pl
from jax.experimental.pallas import tpu as pltpu
from jax.sharding import PartitionSpec as P

ITERS = 4
REACH = 2 * ITERS + 2
MESH = pl.DeviceIdType.MESH
NEIGHBOURS = tuple((dx, dy) for dx in (-1, 0, 1) for dy in (-1, 0, 1) if (dx, dy) != (0, 0))
NT = (((1,), (1,)), ((), ()))
NN = (((1,), (0,)), ((), ()))
C0 = 0.7978845608028654
C1 = 0.044715


def dot(a, b, dims):
    return lax.dot_general(a, b, dims, preferred_element_type=jnp.float32)


def roll_to(x, shift, axis):
    return pltpu.roll(x, shift % x.shape[axis], axis)


def gelu_both(v):
    square = v * v
    half = 0.5 * (1.0 + jnp.tanh(v * (C0 + (C0 * C1) * square)))
    value = v * half
    return value, half + (value * (1.0 - half)) * (2.0 * C0 + (6.0 * C0 * C1) * square)


def fused_kernel(
    nx, ny, factor, cot_in, vel_in, pre1_in, pre2_in, last_in, taps_in, first_in,
    spread_out, middle_out, last_out, first_out, bias1_out, bias2_out,
    cot, far, far_in, cot_edge, cot_side, cot_spot, cot_spot_in, vel, raw, w_lasts, w_taps, w_firsts, natural, rowsend, halo, vel_rows, vel_halo,
    edges, edge_in, spots, spots_in, slots, grads, sums, gathered, few, few_in, adj, vel_wide, vel_band, slope1, slope2, hidden2, hidden3, stacks, partial,
    deltas, w_middle, w_last, w_first, small, gm, border, side_out, row_in, corner_in, side_in,
    send, recv, load, send_all, recv_all,
):
    rows, cols = vel.shape[1], vel.shape[2]
    ch = raw.shape[1]
    wide = cols + 128
    blocks = cols // 128
    band = rows + 16
    f32, bf16 = jnp.float32, jnp.bfloat16
    gx, gy = lax.axis_index("gx"), lax.axis_index("gy")
    count = nx * ny
    me = gx * ny + gy

    loads = [
        pltpu.make_async_copy(src, dst, load.at[i])
        for i, (src, dst) in enumerate((
            (pre2_in, raw.at[1]), (pre1_in, raw.at[0]), (cot_in, cot.at[:, rows : 2 * rows]), (vel_in, vel),
            (taps_in, w_taps), (last_in, w_lasts), (first_in, w_firsts),
        ))
    ]
    for copy in loads:
        copy.start()

    def device(k):
        other = lax.rem(me + k, count)
        return other, (lax.div(other, ny), lax.rem(other, ny))

    for part in (slice(0, 8), slice(3 * rows - 8, 3 * rows)):
        cot[:, part] = jnp.zeros((2, 8, cols), f32)

    barrier = pltpu.get_barrier_semaphore()

    def hail(k, _):
        pl.semaphore_signal(barrier, inc=1, device_id=device(k)[1], device_id_type=MESH)
        return 0

    straight = count - 1 if count <= 64 else 1
    lax.fori_loop(1, count, hail, 0, unroll=straight)

    def at(dx, dy):
        return (lax.rem(gx + dx + nx, nx), lax.rem(gy + dy + ny, ny))

    def remote(src, dst, which, index, peer):
        return pltpu.make_async_remote_copy(
            src_ref=src, dst_ref=dst, send_sem=send.at[which, index], recv_sem=recv.at[which, index],
            device_id=peer, device_id_type=MESH,
        )

    own = slice(rows, 2 * rows)
    cot_copies, edge_copies, back_copies, row_copies = [], [], [], []
    for i, (dx, dy) in enumerate(NEIGHBOURS):
        side, down = (1 + dy) // 2, (1 + dx) // 2
        if dy:
            cot_copies.append(
                remote(cot_spot.at[side], cot_spot_in.at[down, side], 0, i, at(dx, dy)) if dx
                else remote(cot_edge.at[side], cot_side.at[side, own], 0, i, at(dx, dy))
            )
            if dx:
                edge_copies.append(remote(spots.at[down, side], spots_in.at[down, side], 1, i, at(dx, dy)))
            else:
                edge_copies.append(remote(edges.at[side], edge_in.at[side], 1, i, at(dx, dy)))
        else:
            source = {1: slice(2 * rows - 8, 2 * rows), -1: slice(rows, rows + 8)}[dx]
            land = {1: slice(rows - 8, rows), -1: slice(2 * rows, 2 * rows + 8)}[dx]
            cot_copies.append(remote(cot.at[:, source], cot.at[:, land], 0, i, at(dx, dy)))
            cot_copies.append(remote(far.at[down], far_in.at[down], 2, 4 + down, at(dx, dy)))
            row_copies.append(remote(rowsend.at[down], halo.at[down], 2, down, at(dx, dy)))
            row_copies.append(remote(vel_rows.at[down], vel_halo.at[down], 2, 2 + down, at(dx, dy)))
        if dx and dy:
            back_copies.append(
                remote(border.at[down, :, :, cols:wide], corner_in.at[down, side], 3, i, at(dx, dy))
            )
        elif dx:
            back_copies.append(remote(border.at[down, :, :, 0:cols], row_in.at[down], 3, i, at(dx, dy)))
        else:
            back_copies.append(remote(side_out, side_in.at[side], 3, i, at(dx, dy)))
    def to_all(which, source, slot):
        def go(k, _):
            other, peer = device(k)
            pltpu.make_async_remote_copy(
                src_ref=source(other), dst_ref=slot.at[me], send_sem=send_all.at[which],
                recv_sem=recv_all.at[which], device_id=peer, device_id_type=MESH,
            ).start()
            return 0

        lax.fori_loop(1, count, go, 0, unroll=straight)
        most = slot.at[pl.ds(0, count - 1)]
        return pltpu.make_async_remote_copy(
            src_ref=most, dst_ref=most, send_sem=send_all.at[which], recv_sem=recv_all.at[which],
            device_id=at(0, 1), device_id_type=MESH,
        )

    def total_of(slot):
        total = slot[0]
        for k in range(1, count):
            total = total + slot[k]
        return total

    def iota(shape, axis):
        return lax.broadcasted_iota(jnp.int32, shape, axis)

    loads[2].wait()
    lane = iota((rows, 128), 1)
    c_first = [cot[k, own, 0:128] for k in range(2)]
    c_last = [cot[k, own, cols - 128 : cols] for k in range(2)]
    for down, row in ((0, rows + 8), (1, 2 * rows - REACH)):
        for k in range(2):
            for i in range(REACH - 8):
                far[down, (REACH - 8) * k + i] = cot[k, row + i : row + i + 1, :]
    cot_edge[0] = jnp.where(lane < 16, c_first[0], roll_to(c_first[1], 16, 1))
    cot_edge[1] = jnp.where(lane < 112, roll_to(c_last[1], -16, 1), c_last[0])
    low_half, high_half = slice(0, rows // 2), slice(rows // 2, rows)
    lane = iota((rows // 2, 128), 1)
    cot_spot[0] = jnp.where(lane < 32, cot_edge[0, high_half], roll_to(cot_edge[0, low_half], 32, 1))
    cot_spot[1] = jnp.where(lane < 96, roll_to(cot_edge[1, low_half], -32, 1), cot_edge[1, high_half])
    loads[0].wait()
    loads[1].wait()

    def widen(c, _):
        for which in range(2):
            block = raw[which, c].astype(f32)
            for part in range(blocks):
                natural[which, part, pl.ds(c * rows, rows), :] = block[:, 128 * part : 128 * part + 128]
        return 0

    lax.fori_loop(0, ch, widen, 0, unroll=4)

    def row_of(which, part, r):
        return natural[which, part, pl.ds(r, ch, rows), :]

    loads[3].wait()
    v = vel[...].astype(f32)
    for i, r in enumerate((0, rows - 1)):
        for part in range(blocks):
            rowsend[i, :, 128 * part : 128 * part + 128] = row_of(1, part, r).astype(bf16)
        for k in range(2):
            vel_rows[i, k] = v[k, r : r + 1]
    lane = iota((ch, 128), 1)
    placed = iota((rows, 128), 1) == iota((rows, 128), 0) + 1
    diagonal = iota((ch + 16, 128), 0) == iota((ch + 16, 128), 1)
    for side in range(2):
        built = jnp.zeros((ch, 128), f32)
        for r in range(rows):
            moved = roll_to(row_of(1, (blocks - 1) * side, r), r + 1 + side, 1)
            built = jnp.where(lane == r + 1, moved, built)
        col = (cols - 1) * side
        ends = [
            jnp.sum(jnp.where(placed, v[k, :, col : col + 1], 0.0), axis=0, keepdims=True) for k in range(2)
        ]
        built = jnp.concatenate([built] + ends + [jnp.zeros((14, 128), f32)], axis=0)
        edges[side] = built.astype(bf16)
        for down, at_lane in ((0, 1), (1, rows)):
            spots[down, side] = jnp.sum(
                jnp.where(diagonal, built[:, at_lane : at_lane + 1], 0.0), axis=0, keepdims=True
            )

    pl.semaphore_wait(barrier, count - 1)
    for copy in cot_copies:
        copy.start()

    for copy in loads[4:]:
        copy.wait()
    turned = [w_taps[3 * a : 3 * a + 3].astype(f32).reshape(3 * ch, ch) for a in range(3)]
    for a in range(3):
        w_middle[a * ch : (a + 1) * ch, :] = turned[a].T.astype(bf16)
    small[...] = jnp.zeros_like(small)
    for t in range(9):
        small[0, 2 * t : 2 * t + 2, 0:ch] = w_lasts[t].astype(f32)
        small[1, 2 * t : 2 * t + 2, 0:ch] = w_firsts[t].astype(f32)
    taps = iota((32, 256), 0)
    place = iota((32, 256), 1)
    spot = jnp.where((taps < 18) & (place == band * lax.rem(taps, 6) + 8 - lax.div(taps, 6)), 1.0, 0.0)
    w_turned = small[0].T[0:ch, 0:32].astype(bf16)
    base = dot(w_turned, spot.astype(bf16), NN)
    for i in range(rows + 2):
        w_last[i * ch : (i + 1) * ch, :] = (roll_to(base, i, 1) if i else base).astype(bf16)
    taps = iota((256, 32), 1)
    place = iota((256, 32), 0)
    spot = jnp.where((taps < 18) & (place == band * lax.rem(taps, 6) + 7 + lax.div(taps, 6)), 1.0, 0.0)
    base = dot(spot.astype(bf16), small[1, 0:32, 0:ch].astype(bf16), NN)[0 : 6 * band]
    for j in range(0, rows, 2):
        w_first[:, j * ch : (j + 2) * ch] = jnp.concatenate(
            [roll_to(base, j, 0) if j else base, roll_to(base, j + 1, 0)], axis=1
        ).astype(bf16)
    gm[...] = jnp.zeros_like(gm)
    for i, a in ((0, 0), (0, 1), (1, 0), (rows, 2), (rows + 1, 1), (rows + 1, 2)):
        hidden3[i, a * ch : (a + 1) * ch, :] = jnp.zeros((ch, cols), bf16)
    one_row = jnp.where(iota((16, cols), 0) == 0, 1.0, 0.0).astype(bf16)
    for i in range(rows + 2):
        hidden3[i, 3 * ch : 3 * ch + 16, :] = one_row if 0 < i <= rows else jnp.zeros((16, cols), bf16)

    def activate(r, _):
        for part in range(blocks):
            here = slice(128 * part, 128 * part + 128)
            value, slope = gelu_both(row_of(1, part, r))
            hidden2[r, :, here] = value.astype(bf16)
            slope2[r + 1, :, here] = slope
            value, slope = gelu_both(row_of(0, part, r))
            value = value.astype(bf16)
            for a in range(3):
                hidden3[r + 2 - a, a * ch : (a + 1) * ch, here] = value
            slope1[r, :, here] = slope
        return 0

    lax.fori_loop(0, rows, activate, 0)
    for copy in row_copies + edge_copies:
        copy.start()

    for copy in cot_copies:
        copy.wait_recv()
    for down, row in ((1, rows - REACH), (0, 2 * rows + 8)):
        for k in range(2):
            for i in range(REACH - 8):
                cot[k, row + i : row + i + 1, :] = far_in[down, (REACH - 8) * k + i]
    for down, row in ((1, 0), (0, 2 * rows)):
        for side, shift in ((0, -32), (1, 32)):
            spot = cot_spot_in[down, side]
            cot_side[side, row + rows // 2 : row + rows] = spot
            cot_side[side, row : row + rows // 2] = roll_to(spot, shift, 1)
    tall = iota((3 * rows, 128), 1) < 64
    from_right, from_left = cot_side[0], cot_side[1]
    sides = [
        jnp.where(tall, from_right, from_left),
        jnp.where(tall, roll_to(from_right, -16, 1), roll_to(from_left, 16, 1)),
    ]
    c0, c1 = (jnp.concatenate([cot[k], sides[k]], axis=1) for k in range(2))
    rhs = -0.5 * ((roll_to(c0, -1, 0) - roll_to(c0, 1, 0)) + (roll_to(c1, -1, 1) - roll_to(c1, 1, 1)))
    fields = [rhs]
    for _ in range(ITERS):
        q = fields[-1]
        beside = roll_to(q, 2, 0) + roll_to(q, -2, 0) + roll_to(q, 2, 1)
        fields.append(-0.25 * (beside + roll_to(q, -2, 1)))
    inner = [f[own, 0:cols] for f in fields]
    parts = []
    for k in range(2 * ITERS):
        product = inner[k // 2] * inner[(k + 1) // 2]
        total = product[:, 0:128]
        for at_lane in range(128, cols, 128):
            total = total + product[:, at_lane : at_lane + 128]
        parts.append(jnp.sum(total, axis=0, keepdims=True))
    moments = jnp.sum(jnp.concatenate(parts, axis=0), axis=1, keepdims=True)
    square = iota((8, 128), 0) == iota((8, 128), 1)
    slots[me] = jnp.sum(jnp.where(square, moments, 0.0), axis=0, keepdims=True)
    started = to_all(0, lambda other: slots.at[me], slots)

    for copy in row_copies + edge_copies:
        copy.wait_recv()
    tall = iota((ch + 16, 128), 1)
    merged = []
    for side in range(2):
        below, above = (
            jnp.sum(jnp.where(diagonal, spots_in[down, side], 0.0), axis=1, keepdims=True) for down in range(2)
        )
        mid = jnp.where(tall < 1, above, edge_in[side].astype(f32))
        merged.append(jnp.where(tall > rows, below, mid))
    bent = [gelu_both(m[0:ch])[1] for m in merged]
    for i in range(rows + 2):
        slope2[i, :, cols:wide] = jnp.where(
            lane < 64, roll_to(bent[0], -i, 1) if i else bent[0], roll_to(bent[1], 127 - i, 1)
        )
    for i, row in ((1, 0), (0, rows + 1)):
        slope2[row, :, 0:cols] = gelu_both(halo[i].astype(f32))[1]
    vel_wide[...] = jnp.zeros_like(vel_wide)
    vel_wide[:, 8 : 8 + rows, 0:cols] = v
    upright = [roll_to(m[ch : ch + 16].T[0:band], 7, 0) for m in merged]
    at_lane = iota((band, 128), 1)
    for k in range(2):
        vel_wide[k, :, cols:wide] = jnp.where(at_lane == 0, upright[0][:, k : k + 1], 0.0) + jnp.where(
            at_lane == 127, upright[1][:, k : k + 1], 0.0
        )
        for i, row in ((1, 7), (0, 8 + rows)):
            vel_wide[k, row : row + 1, 0:cols] = vel_halo[i, k]
    for b in (-1, 0, 1):
        for k in range(2):
            at_band = band * (2 * (b + 1) + k)
            moved = roll_to(vel_wide[k], -b, 1) if b else vel_wide[k]
            vel_band[at_band : at_band + band, :] = moved[:, 0:cols].astype(bf16)
    vel_band[6 * band : 256, :] = jnp.where(iota((256 - 6 * band, cols), 0) < rows, 1.0, 0.0).astype(bf16)

    started.wait_recv()
    moments = jnp.sum(jnp.where(square, jnp.sum(slots[...], axis=0), 0.0), axis=1, keepdims=True)
    n = [moments[k : k + 1, 0:1] for k in range(2 * ITERS)]
    zero, one = jnp.zeros_like(n[0]), jnp.ones_like(n[0])
    lam, residual, direction = [zero] * (ITERS + 1), [one] + [zero] * ITERS, [one] + [zero] * ITERS
    norm_now = n[0]
    sums_of_two = [n[k] + n[k + 1] for k in range(2 * ITERS - 1)]

    def against(weights, moments):
        terms = []
        for m in range(2 * len(weights) - 1):
            for i in range(max(0, m - len(weights) + 1), m // 2 + 1):
                twice = weights[i] * weights[m - i]
                terms.append((twice if 2 * i == m else twice + twice) * moments[m])
        while len(terms) > 1:
            terms = [sum(terms[k + 1 : k + 2], terms[k]) for k in range(0, len(terms), 2)]
        return terms[0]

    for step in range(ITERS):
        alpha = norm_now / against(direction[: step + 1], sums_of_two)
        lam = [x + alpha * p for x, p in zip(lam, direction)]
        if step + 1 < ITERS:
            image = [p + below for p, below in zip(direction, [zero] + direction[:-1])]
            residual = [r - alpha * a for r, a in zip(residual, image)]
            norm_next = against(residual[: step + 2], n)
            ratio = norm_next / norm_now
            direction = [r + ratio * p for r, p in zip(residual, direction)]
            norm_now = norm_next
    field = lam[0] * fields[0]
    for k in range(1, ITERS):
        field = field + lam[k] * fields[k]
    low = rows - 8
    a0 = (c0 + 0.5 * (roll_to(field, 1, 0) - roll_to(field, -1, 0)))[low : low + band]
    a1 = (c1 + 0.5 * (roll_to(field, 1, 1) - roll_to(field, -1, 1)))[low : low + band]
    adj[0] = a0[8 : 8 + rows, 0:cols]
    adj[1] = a1[8 : 8 + rows, 0:cols]
    banded = jnp.concatenate(
        [roll_to(x, b, 1) if b else x for b in (-1, 0, 1) for x in (a0, a1)]
        + [jnp.zeros((256 - 6 * band, wide), f32)],
        axis=0,
    ).astype(bf16)

    flat = dot(w_last[...], banded, NN)
    for i in range(rows + 2):
        narrow = (flat[i * ch : (i + 1) * ch] * slope2[i]).astype(bf16)
        for at_b, b in enumerate((-1, 0, 1)):
            moved = roll_to(narrow, b, 1) if b else narrow
            stacks[i, at_b * ch : (at_b + 1) * ch, :] = moved[:, 0:cols]
    for i in range(0, rows + 2, 2):
        gm[...] += dot(
            jnp.concatenate([stacks[i], stacks[i + 1]], axis=1),
            jnp.concatenate([hidden3[i], hidden3[i + 1]], axis=1), NT,
        )

    def fold(source, other):
        flat = dot(source[...].reshape(rows * ch, cols), other, NT)
        total = flat[0:ch]
        for r in range(1, rows):
            total = total + roll_to(flat[r * ch : (r + 1) * ch], -r, 1)
        return total

    half = 9 * ch // 2
    chunk = grads.shape[1]
    third = 3 * ch // 2
    packed = jnp.concatenate([gm[0:third, 128:192], gm[third : 2 * third, 128:192]], axis=1)
    packed = [gm[:, 0:128], packed]
    if count * chunk > half:
        packed.append(jnp.zeros((count * chunk - half, 128), f32))
    packed = jnp.concatenate(packed, axis=0)
    for k in range(count):
        grads[k] = packed[k * chunk : (k + 1) * chunk]
    sums[me] = grads[me]
    scatter = to_all(1, lambda other: grads.at[other], sums)

    for i in range(0, rows + 2, 2):
        flat = dot(w_middle[...], jnp.concatenate([stacks[i], stacks[i + 1]], axis=1), NN)
        partial[i] = flat[:, 0:cols]
        partial[i + 1] = flat[:, cols : 2 * cols]
    for j in range(rows):
        total = partial[j + 2, 0:ch] + partial[j + 1, ch : 2 * ch] + partial[j, 2 * ch : 3 * ch]
        deltas[j] = (total * slope1[j]).astype(bf16)
    gf = fold(deltas, vel_band[...])
    gl = fold(hidden2, banded[:, 0:cols])
    gl = jnp.where(iota((ch, 256), 1) == 6 * band, gm[ch : 2 * ch, 3 * ch : 3 * ch + 1], gl)
    folded = jnp.concatenate([gf, gl], axis=0).T
    few[...] = jnp.zeros_like(few)
    for m in range(19):
        here = [6 * band if m == 18 else band * (m % 6) + 8 + sign * (m // 6 - 1) for sign in (1, -1)]
        few[m, :, 0:ch] = folded[here[0] : here[0] + 1, 0:ch]
        few[m, :, ch : 2 * ch] = folded[here[1] : here[1] + 1, ch : 2 * ch]
    few_in[me] = few[me]
    last = to_all(3, lambda other: few.at[other], few_in)
    flat = dot(w_first[...], deltas[...].reshape(rows * ch, cols), NN)
    flat = jnp.concatenate([flat, jnp.zeros((6 * band, 128), f32)], axis=1)
    spread = []
    for k in range(2):
        terms = [flat[band * (2 * s + k) : band * (2 * s + k + 1)] for s in range(3)]
        spread.append(roll_to(terms[0], -1, 1) + terms[1] + roll_to(terms[2], 1, 1))
        border[0, k] = spread[k][7:8]
        border[1, k] = spread[k][8 + rows : 9 + rows]
        side_out[k] = spread[k][8 : 8 + rows, cols:wide]
    for copy in back_copies:
        copy.start()
    for k in range(2):
        spread_out[k] = adj[k] + spread[k][8 : 8 + rows, 0:cols]
    for copy in cot_copies + edge_copies + row_copies:
        copy.wait_send()
    started.wait_send()

    scatter.wait_recv()
    blank = jnp.zeros((gathered.shape[1] - chunk - 1, 128), f32)
    scattered = total_of(sums)
    last.wait_recv()
    reduced = jnp.concatenate([scattered, total_of(few_in), blank], axis=0)
    gathered[me] = (factor * reduced).astype(bf16)
    spreading = to_all(2, lambda other: gathered.at[me], gathered)
    for copy in back_copies:
        copy.wait_recv()
    for copy in back_copies:
        copy.wait_send()
    left = iota((1, 128), 1) == 0
    right = iota((1, 128), 1) == 127
    for k in range(2):
        spread_out[k, :, 0:128] += jnp.where(left, side_in[1, k], 0.0)
        spread_out[k, :, cols - 128 : cols] += jnp.where(right, side_in[0, k], 0.0)
        for down, row in ((1, 0), (0, rows - 1)):
            spread_out[k, row : row + 1, :] += row_in[down, k]
            spread_out[k, row : row + 1, 0:128] += jnp.where(left, corner_in[down, 1, k], 0.0)
            spread_out[k, row : row + 1, cols - 128 : cols] += jnp.where(right, corner_in[down, 0, k], 0.0)
    scatter.wait_send()
    last.wait_send()
    spreading.wait_recv()
    spreading.wait_send()
    arrived = [gathered[k].astype(f32) for k in range(count)]
    whole = jnp.concatenate([x[0:chunk] for x in arrived], axis=0)
    for t in range(9):
        a, start = t // 3, (t % 3) * ch
        for low in range(0, ch, 32):
            here = start + low
            side = a * ch
            if a == 2:
                side = 0 if here < third else 64
                here = 3 * ch + here % third
            middle_out[t, low : low + 32, :] = whole[here : here + 32, side : side + ch]
    for t in range(9):
        for k in range(2):
            pair = arrived[2 * t + k][chunk : chunk + 1]
            first_out[t, k : k + 1] = pair[:, 0:ch]
            last_out[t, k : k + 1] = pair[:, ch : 2 * ch]
    pair = arrived[18][chunk : chunk + 1]
    bias1_out[...] = pair[:, 0:ch]
    bias2_out[...] = pair[:, ch : 2 * ch]


def store_kernel(*refs):
    count = (len(refs) - 1) // 2
    copies = [
        pltpu.make_async_copy(refs[i], refs[count + i], refs[-1].at[i]) for i in range(count)
    ]
    for copy in copies:
        copy.start()
    for copy in copies:
        copy.wait()


def per_device(nx, ny, cotangent, velocity_in, hidden_pre1, hidden_pre2, w_first, w_middle, w_last):
    rows, cols = cotangent.shape[1], cotangent.shape[2]
    ch = hidden_pre1.shape[0]
    f32, bf16 = jnp.float32, jnp.bfloat16
    factor = 1.0 / math.sqrt(rows * nx * cols * ny)
    vmem = pl.BlockSpec(memory_space=pltpu.VMEM)
    anywhere = pl.BlockSpec(memory_space=pl.ANY)
    dma = pltpu.SemaphoreType.DMA
    count = nx * ny
    chunk = -(-(9 * ch // 2) // count)
    wide, band = cols + 128, rows + 16
    out_shapes = (
        jax.ShapeDtypeStruct((2, rows, cols), f32),
        jax.ShapeDtypeStruct((9, ch, ch), f32),
        jax.ShapeDtypeStruct((9, 2, ch), f32),
        jax.ShapeDtypeStruct((9, 2, ch), f32),
        jax.ShapeDtypeStruct((1, ch), f32),
        jax.ShapeDtypeStruct((1, ch), f32),
    )
    results = pl.pallas_call(
        functools.partial(fused_kernel, nx, ny, factor),
        out_shape=out_shapes,
        in_specs=[anywhere] * 7,
        out_specs=(vmem,) * 6,
        scratch_shapes=[
            pltpu.VMEM((2, 3 * rows, cols), f32),
            pltpu.VMEM((2, 2 * (REACH - 8), 1, cols), f32),
            pltpu.VMEM((2, 2 * (REACH - 8), 1, cols), f32),
            pltpu.VMEM((2, rows, 128), f32),
            pltpu.VMEM((2, 3 * rows, 128), f32),
            pltpu.VMEM((2, rows // 2, 128), f32),
            pltpu.VMEM((2, 2, rows // 2, 128), f32),
            pltpu.VMEM((2, rows, cols), bf16),
            pltpu.VMEM((2, ch, rows, cols), bf16),
            pltpu.VMEM((9, 2, ch), bf16),
            pltpu.VMEM((9, ch, ch), bf16),
            pltpu.VMEM((9, 2, ch), bf16),
            pltpu.VMEM((2, cols // 128, ch * rows, 128), f32),
            pltpu.VMEM((2, ch, cols), bf16),
            pltpu.VMEM((2, ch, cols), bf16),
            pltpu.VMEM((2, 2, 1, cols), f32),
            pltpu.VMEM((2, 2, 1, cols), f32),
            pltpu.VMEM((2, ch + 16, 128), bf16),
            pltpu.VMEM((2, ch + 16, 128), bf16),
            pltpu.VMEM((2, 2, 1, 128), f32),
            pltpu.VMEM((2, 2, 1, 128), f32),
            pltpu.VMEM((count, 1, 128), f32),
            pltpu.VMEM((count, chunk, 128), f32),
            pltpu.VMEM((count, chunk, 128), f32),
            pltpu.VMEM((count, 16 * (-(-(chunk + 1) // 16)), 128), bf16),
            pltpu.VMEM((count, 1, 128), f32),
            pltpu.VMEM((count, 1, 128), f32),
            pltpu.VMEM((2, rows, cols), f32),
            pltpu.VMEM((2, band, wide), f32),
            pltpu.VMEM((256, cols), bf16),
            pltpu.VMEM((rows, ch, cols), f32),
            pltpu.VMEM((rows + 2, ch, wide), f32),
            pltpu.VMEM((rows, ch, cols), bf16),
            pltpu.VMEM((rows + 2, 3 * ch + 16, cols), bf16),
            pltpu.VMEM((rows + 2, 3 * ch, cols), bf16),
            pltpu.VMEM((rows + 2, 3 * ch, cols), f32),
            pltpu.VMEM((rows, ch, cols), bf16),
            pltpu.VMEM((3 * ch, 3 * ch), bf16),
            pltpu.VMEM(((rows + 2) * ch, 256), bf16),
            pltpu.VMEM((6 * band, rows * ch), bf16),
            pltpu.VMEM((2, 128, 128), f32),
            pltpu.VMEM((3 * ch, 3 * ch + 16), f32),
            pltpu.VMEM((2, 2, 1, wide), f32),
            pltpu.VMEM((2, rows, 128), f32),
            pltpu.VMEM((2, 2, 1, cols), f32),
            pltpu.VMEM((2, 2, 2, 1, 128), f32),
            pltpu.VMEM((2, 2, rows, 128), f32),
            dma((4, 8)), dma((4, 8)), dma((7,)), dma((4,)), dma((4,)),
        ],
        compiler_params=pltpu.CompilerParams(
            collective_id=0, has_side_effects=True, vmem_limit_bytes=56 * 2**20
        ),
    )(
        cotangent, velocity_in, hidden_pre1, hidden_pre2, w_last, w_middle, jnp.transpose(w_first, (0, 2, 1)),
    )
    grad_velocity, grad_middle, grad_last, grad_first, bias1, bias2 = pl.pallas_call(
        store_kernel,
        out_shape=out_shapes,
        in_specs=[vmem] * 6,
        out_specs=(anywhere,) * 6,
        scratch_shapes=[dma((6,))],
    )(*results)
    grad_first = jnp.transpose(grad_first, (0, 2, 1))
    return grad_velocity, grad_first, grad_middle, grad_last, bias1.reshape(ch), bias2.reshape(ch)


def solution(mesh):
    whole = P(None, "gx", "gy")
    return jax.shard_map(
        functools.partial(per_device, mesh.shape["gx"], mesh.shape["gy"]),
        mesh=mesh,
        in_specs=(whole, whole, whole, whole, P(), P(), P()),
        out_specs=(whole, P(), P(), P(), P(), P()),
        check_vma=False,
    )
```

```python
import functools
import math

import jax
import jax.numpy as jnp
from jax import lax
from jax.experimental import pallas as pl
from jax.experimental.pallas import tpu as pltpu
from jax.sharding import PartitionSpec as P

ITERS = 4
REACH = 2 * ITERS + 2
MESH = pl.DeviceIdType.MESH
NEIGHBOURS = tuple((dx, dy) for dx in (-1, 0, 1) for dy in (-1, 0, 1) if (dx, dy) != (0, 0))
NT = (((1,), (1,)), ((), ()))
NN = (((1,), (0,)), ((), ()))
C0 = 0.7978845608028654
C1 = 0.044715


def dot(a, b, dims):
    return lax.dot_general(a, b, dims, preferred_element_type=jnp.float32)


def roll_to(x, shift, axis):
    return pltpu.roll(x, shift % x.shape[axis], axis)


def gelu_both(v):
    square = v * v
    half = 0.5 * (1.0 + jnp.tanh(v * (C0 + (C0 * C1) * square)))
    value = v * half
    return value, half + (value * (1.0 - half)) * (2.0 * C0 + (6.0 * C0 * C1) * square)


def fused_kernel(
    nx, ny, factor, cot_in, vel_in, pre1_in, pre2_in, last_in, taps_in, first_in,
    spread_out, middle_out, last_out, first_out, bias1_out, bias2_out,
    cot, far, far_in, cot_edge, cot_side, cot_spot, cot_spot_in, vel, raw, w_lasts, w_taps, w_firsts, natural, rowsend, halo, vel_rows, vel_halo,
    edges, edge_in, spots, spots_in, slots, grads, sums, gathered, few, few_in, adj, vel_wide, vel_band, slope1, slope2, hidden2, hidden3, stacks, partial,
    deltas, w_middle, w_last, w_first, small, gm, border, side_out, row_in, corner_in, side_in,
    send, recv, load, send_all, recv_all,
):
    rows, cols = vel.shape[1], vel.shape[2]
    ch = raw.shape[1]
    wide = cols + 128
    blocks = cols // 128
    band = rows + 16
    f32, bf16 = jnp.float32, jnp.bfloat16
    gx, gy = lax.axis_index("gx"), lax.axis_index("gy")
    count = nx * ny
    me = gx * ny + gy

    loads = [
        pltpu.make_async_copy(src, dst, load.at[i])
        for i, (src, dst) in enumerate((
            (cot_in, cot.at[:, rows : 2 * rows]), (pre2_in, raw.at[1]), (vel_in, vel), (pre1_in, raw.at[0]),
            (taps_in, w_taps), (last_in, w_lasts), (first_in, w_firsts),
        ))
    ]
    for copy in loads:
        copy.start()

    def device(k):
        other = lax.rem(me + k, count)
        return other, (lax.div(other, ny), lax.rem(other, ny))

    for part in (slice(0, 8), slice(3 * rows - 8, 3 * rows)):
        cot[:, part] = jnp.zeros((2, 8, cols), f32)

    barrier = pltpu.get_barrier_semaphore()

    def hail(k, _):
        pl.semaphore_signal(barrier, inc=1, device_id=device(k)[1], device_id_type=MESH)
        return 0

    straight = count - 1 if count <= 64 else 1
    lax.fori_loop(1, count, hail, 0, unroll=straight)

    def at(dx, dy):
        return (lax.rem(gx + dx + nx, nx), lax.rem(gy + dy + ny, ny))

    def remote(src, dst, which, index, peer):
        return pltpu.make_async_remote_copy(
            src_ref=src, dst_ref=dst, send_sem=send.at[which, index], recv_sem=recv.at[which, index],
            device_id=peer, device_id_type=MESH,
        )

    own = slice(rows, 2 * rows)
    cot_copies, edge_copies, back_copies, row_copies = [], [], [], []
    for i, (dx, dy) in enumerate(NEIGHBOURS):
        side, down = (1 + dy) // 2, (1 + dx) // 2
        if dy:
            cot_copies.append(
                remote(cot_spot.at[side], cot_spot_in.at[down, side], 0, i, at(dx, dy)) if dx
                else remote(cot_edge.at[side], cot_side.at[side, own], 0, i, at(dx, dy))
            )
            if dx:
                edge_copies.append(remote(spots.at[down, side], spots_in.at[down, side], 1, i, at(dx, dy)))
            else:
                edge_copies.append(remote(edges.at[side], edge_in.at[side], 1, i, at(dx, dy)))
        else:
            source = {1: slice(2 * rows - 8, 2 * rows), -1: slice(rows, rows + 8)}[dx]
            land = {1: slice(rows - 8, rows), -1: slice(2 * rows, 2 * rows + 8)}[dx]
            cot_copies.append(remote(cot.at[:, source], cot.at[:, land], 0, i, at(dx, dy)))
            cot_copies.append(remote(far.at[down], far_in.at[down], 2, 4 + down, at(dx, dy)))
            row_copies.append(remote(rowsend.at[down], halo.at[down], 2, down, at(dx, dy)))
            row_copies.append(remote(vel_rows.at[down], vel_halo.at[down], 2, 2 + down, at(dx, dy)))
        if dx and dy:
            back_copies.append(
                remote(border.at[down, :, :, cols:wide], corner_in.at[down, side], 3, i, at(dx, dy))
            )
        elif dx:
            back_copies.append(remote(border.at[down, :, :, 0:cols], row_in.at[down], 3, i, at(dx, dy)))
        else:
            back_copies.append(remote(side_out, side_in.at[side], 3, i, at(dx, dy)))
    def to_all(which, source, slot):
        def go(k, _):
            other, peer = device(k)
            pltpu.make_async_remote_copy(
                src_ref=source(other), dst_ref=slot.at[me], send_sem=send_all.at[which],
                recv_sem=recv_all.at[which], device_id=peer, device_id_type=MESH,
            ).start()
            return 0

        lax.fori_loop(1, count, go, 0, unroll=straight)
        most = slot.at[pl.ds(0, count - 1)]
        return pltpu.make_async_remote_copy(
            src_ref=most, dst_ref=most, send_sem=send_all.at[which], recv_sem=recv_all.at[which],
            device_id=at(0, 1), device_id_type=MESH,
        )

    def total_of(slot):
        total = slot[0]
        for k in range(1, count):
            total = total + slot[k]
        return total

    def iota(shape, axis):
        return lax.broadcasted_iota(jnp.int32, shape, axis)

    loads[0].wait()
    lane = iota((rows, 128), 1)
    c_first = [cot[k, own, 0:128] for k in range(2)]
    c_last = [cot[k, own, cols - 128 : cols] for k in range(2)]
    for down, row in ((0, rows + 8), (1, 2 * rows - REACH)):
        for k in range(2):
            for i in range(REACH - 8):
                far[down, (REACH - 8) * k + i] = cot[k, row + i : row + i + 1, :]
    cot_edge[0] = jnp.where(lane < 16, c_first[0], roll_to(c_first[1], 16, 1))
    cot_edge[1] = jnp.where(lane < 112, roll_to(c_last[1], -16, 1), c_last[0])
    low_half, high_half = slice(0, rows // 2), slice(rows // 2, rows)
    lane = iota((rows // 2, 128), 1)
    cot_spot[0] = jnp.where(lane < 32, cot_edge[0, high_half], roll_to(cot_edge[0, low_half], 32, 1))
    cot_spot[1] = jnp.where(lane < 96, roll_to(cot_edge[1, low_half], -32, 1), cot_edge[1, high_half])
    loads[1].wait()
    loads[3].wait()

    def widen(c, _):
        for which in range(2):
            block = raw[which, c].astype(f32)
            for part in range(blocks):
                natural[which, part, pl.ds(c * rows, rows), :] = block[:, 128 * part : 128 * part + 128]
        return 0

    lax.fori_loop(0, ch, widen, 0, unroll=4)

    def row_of(which, part, r):
        return natural[which, part, pl.ds(r, ch, rows), :]

    loads[2].wait()
    v = vel[...].astype(f32)
    for i, r in enumerate((0, rows - 1)):
        for part in range(blocks):
            rowsend[i, :, 128 * part : 128 * part + 128] = row_of(1, part, r).astype(bf16)
        for k in range(2):
            vel_rows[i, k] = v[k, r : r + 1]
    lane = iota((ch, 128), 1)
    placed = iota((rows, 128), 1) == iota((rows, 128), 0) + 1
    diagonal = iota((ch + 16, 128), 0) == iota((ch + 16, 128), 1)
    for side in range(2):
        built = jnp.zeros((ch, 128), f32)
        for r in range(rows):
            moved = roll_to(row_of(1, (blocks - 1) * side, r), r + 1 + side, 1)
            built = jnp.where(lane == r + 1, moved, built)
        col = (cols - 1) * side
        ends = [
            jnp.sum(jnp.where(placed, v[k, :, col : col + 1], 0.0), axis=0, keepdims=True) for k in range(2)
        ]
        built = jnp.concatenate([built] + ends + [jnp.zeros((14, 128), f32)], axis=0)
        edges[side] = built.astype(bf16)
        for down, at_lane in ((0, 1), (1, rows)):
            spots[down, side] = jnp.sum(
                jnp.where(diagonal, built[:, at_lane : at_lane + 1], 0.0), axis=0, keepdims=True
            )

    pl.semaphore_wait(barrier, count - 1)
    for copy in cot_copies:
        copy.start()

    for copy in loads[4:]:
        copy.wait()
    turned = [w_taps[3 * a : 3 * a + 3].astype(f32).reshape(3 * ch, ch) for a in range(3)]
    for a in range(3):
        w_middle[a * ch : (a + 1) * ch, :] = turned[a].T.astype(bf16)
    small[...] = jnp.zeros_like(small)
    for t in range(9):
        small[0, 2 * t : 2 * t + 2, 0:ch] = w_lasts[t].astype(f32)
        small[1, 2 * t : 2 * t + 2, 0:ch] = w_firsts[t].astype(f32)
    taps = iota((32, 256), 0)
    place = iota((32, 256), 1)
    spot = jnp.where((taps < 18) & (place == band * lax.rem(taps, 6) + 8 - lax.div(taps, 6)), 1.0, 0.0)
    w_turned = small[0].T[0:ch, 0:32].astype(bf16)
    base = dot(w_turned, spot.astype(bf16), NN)
    for i in range(rows + 2):
        w_last[i * ch : (i + 1) * ch, :] = (roll_to(base, i, 1) if i else base).astype(bf16)
    taps = iota((256, 32), 1)
    place = iota((256, 32), 0)
    spot = jnp.where((taps < 18) & (place == band * lax.rem(taps, 6) + 7 + lax.div(taps, 6)), 1.0, 0.0)
    base = dot(spot.astype(bf16), small[1, 0:32, 0:ch].astype(bf16), NN)[0 : 6 * band]
    for j in range(0, rows, 2):
        w_first[:, j * ch : (j + 2) * ch] = jnp.concatenate(
            [roll_to(base, j, 0) if j else base, roll_to(base, j + 1, 0)], axis=1
        ).astype(bf16)
    gm[...] = jnp.zeros_like(gm)
    for i, a in ((0, 0), (0, 1), (1, 0), (rows, 2), (rows + 1, 1), (rows + 1, 2)):
        hidden3[i, a * ch : (a + 1) * ch, :] = jnp.zeros((ch, cols), bf16)
    one_row = jnp.where(iota((16, cols), 0) == 0, 1.0, 0.0).astype(bf16)
    for i in range(rows + 2):
        hidden3[i, 3 * ch : 3 * ch + 16, :] = one_row if 0 < i <= rows else jnp.zeros((16, cols), bf16)

    def activate(r, _):
        for part in range(blocks):
            here = slice(128 * part, 128 * part + 128)
            value, slope = gelu_both(row_of(1, part, r))
            hidden2[r, :, here] = value.astype(bf16)
            slope2[r + 1, :, here] = slope
            value, slope = gelu_both(row_of(0, part, r))
            value = value.astype(bf16)
            for a in range(3):
                hidden3[r + 2 - a, a * ch : (a + 1) * ch, here] = value
            slope1[r, :, here] = slope
        return 0

    lax.fori_loop(0, rows, activate, 0)
    for copy in row_copies + edge_copies:
        copy.start()

    for copy in cot_copies:
        copy.wait_recv()
    for down, row in ((1, rows - REACH), (0, 2 * rows + 8)):
        for k in range(2):
            for i in range(REACH - 8):
                cot[k, row + i : row + i + 1, :] = far_in[down, (REACH - 8) * k + i]
    for down, row in ((1, 0), (0, 2 * rows)):
        for side, shift in ((0, -32), (1, 32)):
            spot = cot_spot_in[down, side]
            cot_side[side, row + rows // 2 : row + rows] = spot
            cot_side[side, row : row + rows // 2] = roll_to(spot, shift, 1)
    tall = iota((3 * rows, 128), 1) < 64
    from_right, from_left = cot_side[0], cot_side[1]
    sides = [
        jnp.where(tall, from_right, from_left),
        jnp.where(tall, roll_to(from_right, -16, 1), roll_to(from_left, 16, 1)),
    ]
    c0, c1 = (jnp.concatenate([cot[k], sides[k]], axis=1) for k in range(2))
    rhs = -0.5 * ((roll_to(c0, -1, 0) - roll_to(c0, 1, 0)) + (roll_to(c1, -1, 1) - roll_to(c1, 1, 1)))
    fields = [rhs]
    for _ in range(ITERS):
        q = fields[-1]
        beside = roll_to(q, 2, 0) + roll_to(q, -2, 0) + roll_to(q, 2, 1)
        fields.append(-0.25 * (beside + roll_to(q, -2, 1)))
    inner = [f[own, 0:cols] for f in fields]
    parts = []
    for k in range(2 * ITERS):
        product = inner[k // 2] * inner[(k + 1) // 2]
        total = product[:, 0:128]
        for at_lane in range(128, cols, 128):
            total = total + product[:, at_lane : at_lane + 128]
        parts.append(jnp.sum(total, axis=0, keepdims=True))
    moments = jnp.sum(jnp.concatenate(parts, axis=0), axis=1, keepdims=True)
    square = iota((8, 128), 0) == iota((8, 128), 1)
    slots[me] = jnp.sum(jnp.where(square, moments, 0.0), axis=0, keepdims=True)
    started = to_all(0, lambda other: slots.at[me], slots)

    for copy in row_copies + edge_copies:
        copy.wait_recv()
    tall = iota((ch + 16, 128), 1)
    merged = []
    for side in range(2):
        below, above = (
            jnp.sum(jnp.where(diagonal, spots_in[down, side], 0.0), axis=1, keepdims=True) for down in range(2)
        )
        mid = jnp.where(tall < 1, above, edge_in[side].astype(f32))
        merged.append(jnp.where(tall > rows, below, mid))
    bent = [gelu_both(m[0:ch])[1] for m in merged]
    for i in range(rows + 2):
        slope2[i, :, cols:wide] = jnp.where(
            lane < 64, roll_to(bent[0], -i, 1) if i else bent[0], roll_to(bent[1], 127 - i, 1)
        )
    for i, row in ((1, 0), (0, rows + 1)):
        slope2[row, :, 0:cols] = gelu_both(halo[i].astype(f32))[1]
    vel_wide[...] = jnp.zeros_like(vel_wide)
    vel_wide[:, 8 : 8 + rows, 0:cols] = v
    upright = [roll_to(m[ch : ch + 16].T[0:band], 7, 0) for m in merged]
    at_lane = iota((band, 128), 1)
    for k in range(2):
        vel_wide[k, :, cols:wide] = jnp.where(at_lane == 0, upright[0][:, k : k + 1], 0.0) + jnp.where(
            at_lane == 127, upright[1][:, k : k + 1], 0.0
        )
        for i, row in ((1, 7), (0, 8 + rows)):
            vel_wide[k, row : row + 1, 0:cols] = vel_halo[i, k]
    for b in (-1, 0, 1):
        for k in range(2):
            at_band = band * (2 * (b + 1) + k)
            moved = roll_to(vel_wide[k], -b, 1) if b else vel_wide[k]
            vel_band[at_band : at_band + band, :] = moved[:, 0:cols].astype(bf16)
    vel_band[6 * band : 256, :] = jnp.where(iota((256 - 6 * band, cols), 0) < rows, 1.0, 0.0).astype(bf16)

    started.wait_recv()
    moments = jnp.sum(jnp.where(square, jnp.sum(slots[...], axis=0), 0.0), axis=1, keepdims=True)
    n = [moments[k : k + 1, 0:1] for k in range(2 * ITERS)]
    zero, one = jnp.zeros_like(n[0]), jnp.ones_like(n[0])
    lam, residual, direction = [zero] * (ITERS + 1), [one] + [zero] * ITERS, [one] + [zero] * ITERS
    norm_now = n[0]
    sums_of_two = [n[k] + n[k + 1] for k in range(2 * ITERS - 1)]

    def against(weights, moments):
        terms = []
        for m in range(2 * len(weights) - 1):
            for i in range(max(0, m - len(weights) + 1), m // 2 + 1):
                twice = weights[i] * weights[m - i]
                terms.append((twice if 2 * i == m else twice + twice) * moments[m])
        while len(terms) > 1:
            terms = [sum(terms[k + 1 : k + 2], terms[k]) for k in range(0, len(terms), 2)]
        return terms[0]

    for step in range(ITERS):
        alpha = norm_now / against(direction[: step + 1], sums_of_two)
        lam = [x + alpha * p for x, p in zip(lam, direction)]
        if step + 1 < ITERS:
            image = [p + below for p, below in zip(direction, [zero] + direction[:-1])]
            residual = [r - alpha * a for r, a in zip(residual, image)]
            norm_next = against(residual[: step + 2], n)
            ratio = norm_next / norm_now
            direction = [r + ratio * p for r, p in zip(residual, direction)]
            norm_now = norm_next
    field = lam[0] * fields[0]
    for k in range(1, ITERS):
        field = field + lam[k] * fields[k]
    low = rows - 8
    a0 = (c0 + 0.5 * (roll_to(field, 1, 0) - roll_to(field, -1, 0)))[low : low + band]
    a1 = (c1 + 0.5 * (roll_to(field, 1, 1) - roll_to(field, -1, 1)))[low : low + band]
    adj[0] = a0[8 : 8 + rows, 0:cols]
    adj[1] = a1[8 : 8 + rows, 0:cols]
    banded = jnp.concatenate(
        [roll_to(x, b, 1) if b else x for b in (-1, 0, 1) for x in (a0, a1)]
        + [jnp.zeros((256 - 6 * band, wide), f32)],
        axis=0,
    ).astype(bf16)

    flat = dot(w_last[...], banded, NN)
    for i in range(rows + 2):
        narrow = (flat[i * ch : (i + 1) * ch] * slope2[i]).astype(bf16)
        for at_b, b in enumerate((-1, 0, 1)):
            moved = roll_to(narrow, b, 1) if b else narrow
            stacks[i, at_b * ch : (at_b + 1) * ch, :] = moved[:, 0:cols]
    for i in range(0, rows + 2, 2):
        gm[...] += dot(
            jnp.concatenate([stacks[i], stacks[i + 1]], axis=1),
            jnp.concatenate([hidden3[i], hidden3[i + 1]], axis=1), NT,
        )

    def fold(source, other):
        flat = dot(source[...].reshape(rows * ch, cols), other, NT)
        total = flat[0:ch]
        for r in range(1, rows):
            total = total + roll_to(flat[r * ch : (r + 1) * ch], -r, 1)
        return total

    half = 9 * ch // 2
    chunk = grads.shape[1]
    third = 3 * ch // 2
    packed = jnp.concatenate([gm[0:third, 128:192], gm[third : 2 * third, 128:192]], axis=1)
    packed = [gm[:, 0:128], packed]
    if count * chunk > half:
        packed.append(jnp.zeros((count * chunk - half, 128), f32))
    packed = jnp.concatenate(packed, axis=0)
    for k in range(count):
        grads[k] = packed[k * chunk : (k + 1) * chunk]
    sums[me] = grads[me]
    scatter = to_all(1, lambda other: grads.at[other], sums)

    for i in range(0, rows + 2, 2):
        flat = dot(w_middle[...], jnp.concatenate([stacks[i], stacks[i + 1]], axis=1), NN)
        partial[i] = flat[:, 0:cols]
        partial[i + 1] = flat[:, cols : 2 * cols]
    for j in range(rows):
        total = partial[j + 2, 0:ch] + partial[j + 1, ch : 2 * ch] + partial[j, 2 * ch : 3 * ch]
        deltas[j] = (total * slope1[j]).astype(bf16)
    gf = fold(deltas, vel_band[...])
    gl = fold(hidden2, banded[:, 0:cols])
    gl = jnp.where(iota((ch, 256), 1) == 6 * band, gm[ch : 2 * ch, 3 * ch : 3 * ch + 1], gl)
    folded = jnp.concatenate([gf, gl], axis=0).T
    few[...] = jnp.zeros_like(few)
    for m in range(19):
        here = [6 * band if m == 18 else band * (m % 6) + 8 + sign * (m // 6 - 1) for sign in (1, -1)]
        few[m, :, 0:ch] = folded[here[0] : here[0] + 1, 0:ch]
        few[m, :, ch : 2 * ch] = folded[here[1] : here[1] + 1, ch : 2 * ch]
    few_in[me] = few[me]
    last = to_all(3, lambda other: few.at[other], few_in)
    flat = dot(w_first[...], deltas[...].reshape(rows * ch, cols), NN)
    flat = jnp.concatenate([flat, jnp.zeros((6 * band, 128), f32)], axis=1)
    spread = []
    for k in range(2):
        terms = [flat[band * (2 * s + k) : band * (2 * s + k + 1)] for s in range(3)]
        spread.append(roll_to(terms[0], -1, 1) + terms[1] + roll_to(terms[2], 1, 1))
        border[0, k] = spread[k][7:8]
        border[1, k] = spread[k][8 + rows : 9 + rows]
        side_out[k] = spread[k][8 : 8 + rows, cols:wide]
    for copy in back_copies:
        copy.start()
    for k in range(2):
        spread_out[k] = adj[k] + spread[k][8 : 8 + rows, 0:cols]
    for copy in cot_copies + edge_copies + row_copies:
        copy.wait_send()
    started.wait_send()

    scatter.wait_recv()
    blank = jnp.zeros((gathered.shape[1] - chunk - 1, 128), f32)
    scattered = total_of(sums)
    last.wait_recv()
    reduced = jnp.concatenate([scattered, total_of(few_in), blank], axis=0)
    gathered[me] = (factor * reduced).astype(bf16)
    spreading = to_all(2, lambda other: gathered.at[me], gathered)
    for copy in back_copies:
        copy.wait_recv()
    for copy in back_copies:
        copy.wait_send()
    left = iota((1, 128), 1) == 0
    right = iota((1, 128), 1) == 127
    for k in range(2):
        spread_out[k, :, 0:128] += jnp.where(left, side_in[1, k], 0.0)
        spread_out[k, :, cols - 128 : cols] += jnp.where(right, side_in[0, k], 0.0)
        for down, row in ((1, 0), (0, rows - 1)):
            spread_out[k, row : row + 1, :] += row_in[down, k]
            spread_out[k, row : row + 1, 0:128] += jnp.where(left, corner_in[down, 1, k], 0.0)
            spread_out[k, row : row + 1, cols - 128 : cols] += jnp.where(right, corner_in[down, 0, k], 0.0)
    scatter.wait_send()
    last.wait_send()
    spreading.wait_recv()
    spreading.wait_send()
    arrived = [gathered[k].astype(f32) for k in range(count)]
    whole = jnp.concatenate([x[0:chunk] for x in arrived], axis=0)
    for t in range(9):
        a, start = t // 3, (t % 3) * ch
        for low in range(0, ch, 32):
            here = start + low
            side = a * ch
            if a == 2:
                side = 0 if here < third else 64
                here = 3 * ch + here % third
            middle_out[t, low : low + 32, :] = whole[here : here + 32, side : side + ch]
    for t in range(9):
        for k in range(2):
            pair = arrived[2 * t + k][chunk : chunk + 1]
            first_out[t, k : k + 1] = pair[:, 0:ch]
            last_out[t, k : k + 1] = pair[:, ch : 2 * ch]
    pair = arrived[18][chunk : chunk + 1]
    bias1_out[...] = pair[:, 0:ch]
    bias2_out[...] = pair[:, ch : 2 * ch]


def store_kernel(*refs):
    count = (len(refs) - 1) // 2
    copies = [
        pltpu.make_async_copy(refs[i], refs[count + i], refs[-1].at[i]) for i in range(count)
    ]
    for copy in copies:
        copy.start()
    for copy in copies:
        copy.wait()


def per_device(nx, ny, cotangent, velocity_in, hidden_pre1, hidden_pre2, w_first, w_middle, w_last):
    rows, cols = cotangent.shape[1], cotangent.shape[2]
    ch = hidden_pre1.shape[0]
    f32, bf16 = jnp.float32, jnp.bfloat16
    factor = 1.0 / math.sqrt(rows * nx * cols * ny)
    vmem = pl.BlockSpec(memory_space=pltpu.VMEM)
    anywhere = pl.BlockSpec(memory_space=pl.ANY)
    dma = pltpu.SemaphoreType.DMA
    count = nx * ny
    chunk = -(-(9 * ch // 2) // count)
    wide, band = cols + 128, rows + 16
    out_shapes = (
        jax.ShapeDtypeStruct((2, rows, cols), f32),
        jax.ShapeDtypeStruct((9, ch, ch), f32),
        jax.ShapeDtypeStruct((9, 2, ch), f32),
        jax.ShapeDtypeStruct((9, 2, ch), f32),
        jax.ShapeDtypeStruct((1, ch), f32),
        jax.ShapeDtypeStruct((1, ch), f32),
    )
    results = pl.pallas_call(
        functools.partial(fused_kernel, nx, ny, factor),
        out_shape=out_shapes,
        in_specs=[anywhere] * 7,
        out_specs=(vmem,) * 6,
        scratch_shapes=[
            pltpu.VMEM((2, 3 * rows, cols), f32),
            pltpu.VMEM((2, 2 * (REACH - 8), 1, cols), f32),
            pltpu.VMEM((2, 2 * (REACH - 8), 1, cols), f32),
            pltpu.VMEM((2, rows, 128), f32),
            pltpu.VMEM((2, 3 * rows, 128), f32),
            pltpu.VMEM((2, rows // 2, 128), f32),
            pltpu.VMEM((2, 2, rows // 2, 128), f32),
            pltpu.VMEM((2, rows, cols), bf16),
            pltpu.VMEM((2, ch, rows, cols), bf16),
            pltpu.VMEM((9, 2, ch), bf16),
            pltpu.VMEM((9, ch, ch), bf16),
            pltpu.VMEM((9, 2, ch), bf16),
            pltpu.VMEM((2, cols // 128, ch * rows, 128), f32),
            pltpu.VMEM((2, ch, cols), bf16),
            pltpu.VMEM((2, ch, cols), bf16),
            pltpu.VMEM((2, 2, 1, cols), f32),
            pltpu.VMEM((2, 2, 1, cols), f32),
            pltpu.VMEM((2, ch + 16, 128), bf16),
            pltpu.VMEM((2, ch + 16, 128), bf16),
            pltpu.VMEM((2, 2, 1, 128), f32),
            pltpu.VMEM((2, 2, 1, 128), f32),
            pltpu.VMEM((count, 1, 128), f32),
            pltpu.VMEM((count, chunk, 128), f32),
            pltpu.VMEM((count, chunk, 128), f32),
            pltpu.VMEM((count, 16 * (-(-(chunk + 1) // 16)), 128), bf16),
            pltpu.VMEM((count, 1, 128), f32),
            pltpu.VMEM((count, 1, 128), f32),
            pltpu.VMEM((2, rows, cols), f32),
            pltpu.VMEM((2, band, wide), f32),
            pltpu.VMEM((256, cols), bf16),
            pltpu.VMEM((rows, ch, cols), f32),
            pltpu.VMEM((rows + 2, ch, wide), f32),
            pltpu.VMEM((rows, ch, cols), bf16),
            pltpu.VMEM((rows + 2, 3 * ch + 16, cols), bf16),
            pltpu.VMEM((rows + 2, 3 * ch, cols), bf16),
            pltpu.VMEM((rows + 2, 3 * ch, cols), f32),
            pltpu.VMEM((rows, ch, cols), bf16),
            pltpu.VMEM((3 * ch, 3 * ch), bf16),
            pltpu.VMEM(((rows + 2) * ch, 256), bf16),
            pltpu.VMEM((6 * band, rows * ch), bf16),
            pltpu.VMEM((2, 128, 128), f32),
            pltpu.VMEM((3 * ch, 3 * ch + 16), f32),
            pltpu.VMEM((2, 2, 1, wide), f32),
            pltpu.VMEM((2, rows, 128), f32),
            pltpu.VMEM((2, 2, 1, cols), f32),
            pltpu.VMEM((2, 2, 2, 1, 128), f32),
            pltpu.VMEM((2, 2, rows, 128), f32),
            dma((4, 8)), dma((4, 8)), dma((7,)), dma((4,)), dma((4,)),
        ],
        compiler_params=pltpu.CompilerParams(
            collective_id=0, has_side_effects=True, vmem_limit_bytes=56 * 2**20
        ),
    )(
        cotangent, velocity_in, hidden_pre1, hidden_pre2, w_last, w_middle, jnp.transpose(w_first, (0, 2, 1)),
    )
    grad_velocity, grad_middle, grad_last, grad_first, bias1, bias2 = pl.pallas_call(
        store_kernel,
        out_shape=out_shapes,
        in_specs=[vmem] * 6,
        out_specs=(anywhere,) * 6,
        scratch_shapes=[dma((6,))],
    )(*results)
    grad_first = jnp.transpose(grad_first, (0, 2, 1))
    return grad_velocity, grad_first, grad_middle, grad_last, bias1.reshape(ch), bias2.reshape(ch)


def solution(mesh):
    whole = P(None, "gx", "gy")
    return jax.shard_map(
        functools.partial(per_device, mesh.shape["gx"], mesh.shape["gy"]),
        mesh=mesh,
        in_specs=(whole, whole, whole, whole, P(), P(), P()),
        out_specs=(whole, P(), P(), P(), P(), P()),
        check_vma=False,
    )
```
